512 devices in a mesh: gx: 16 (over z, x_lo), gy: 32 (over x_hi, y, core).
Axes of the slice: x: 4 (x_hi: 2, x_lo: 2; x = x_hi * 2 + x_lo), y: 8, z: 8, core: 2. Of those that a mesh axis runs over, the one named last changes fastest.
Arguments:
- features: bfloat16 [16, 32, 1600, 128], P('gx', 'gy'), may hold values from -6 to 6
- cotangent: bfloat16 [16, 32, 1600, 128], P('gx', 'gy'), may hold values from -6 to 6
- w_order0: bfloat16 [320, 320], replicated, may hold values from -0.3125 to 0.3125
- w_order1: bfloat16 [2, 256, 256], replicated, may hold values from -0.375 to 0.375
- w_order2: bfloat16 [2, 192, 192], replicated, may hold values from -0.4375 to 0.4375
- w_order3: bfloat16 [2, 128, 128], replicated, may hold values from -0.5 to 0.5
- w_order4: bfloat16 [2, 64, 64], replicated, may hold values from -0.75 to 0.75
- to_grid: float32 [100, 25], replicated, may hold values from -1.25 to 1.25
- from_grid: float32 [25, 100], replicated, may hold values from -0.625 to 0.625
- edge_harmonics: float32 [16, 32, 25, 256], P('gx', 'gy'), may hold values from -5 to 5
- edge_source: int32 [16, 32, 256], P('gx', 'gy'), may hold values from 0 to 383, as said below
- edge_target: int32 [16, 32, 256], P('gx', 'gy'), may hold values from 0 to 128, as said below
- send_list: int32 [16, 32, 8, 32], P('gx', 'gy'), may hold values from 0 to 127, as said below
Outputs:
- layer_out: bfloat16 [16, 32, 1600, 128], P('gx', 'gy')
- feature_grad: float32 [16, 32, 1600, 128], P('gx', 'gy')
The draws below stay inside these ranges and needn't reach their ends.
Inputs may be any that keep to these rules, and one draw needn't show every extreme that they name: `edge_source`: on each cell the live edges come first and padding follows; the number of live edges of a cell is at least 128, and all 256 slots are live on some cell in every draw. Columns below 128 are owned atoms, column 128 + d * 32 + i is entry i of ghost block d. `edge_target`: the value 128 marks a padded edge slot, exactly those slots after a cell's live edges. `send_list`: the 32 entries of one cell and one direction are distinct.
All inputs are finite; a program needn't handle non-finite values.
Results may differ from the reference program's by a relative error of at most 0.0034.
Values may be sent and summed in bfloat16 or wider, within the bound.
A program may use at most 64 MiB of HBM per device.

```python
import jax
import jax.numpy as jnp
from jax import lax

CH = 64
GRID = 100
ATOM_DEV = 128
EDGE_BLOCK = 128
EDGE_DEV = 256
GHOST = 32
N_GX = 16
N_GY = 32


def edge_layout(key):
    base = jax.random.fold_in(key, 11)
    subkeys = jax.random.split(base, 6)
    cell_count = N_GX * N_GY
    uniform_pick = jax.random.randint(subkeys[0], (cell_count,), 0, 1001)
    fraction = uniform_pick * uniform_pick * uniform_pick // 1000000
    minimum = EDGE_BLOCK
    live_edges = minimum + (EDGE_DEV - minimum) * fraction // 1000
    fullest = jax.random.randint(subkeys[1], (), 0, cell_count)
    live_edges = jnp.where(jnp.arange(cell_count) == fullest, EDGE_DEV, live_edges)
    slot_ids = jnp.arange(EDGE_DEV)[None, :]
    is_live = slot_ids < live_edges[:, None]
    shape = (cell_count, EDGE_DEV)
    targets = jax.random.randint(subkeys[2], shape, 0, ATOM_DEV)
    targets = jnp.where(is_live, targets, ATOM_DEV)
    from_ghost = jax.random.randint(subkeys[3], shape, 0, 5) < 2
    own_source = jax.random.randint(subkeys[4], shape, 0, ATOM_DEV)
    ghost_source = ATOM_DEV + jax.random.randint(subkeys[5], shape, 0, 8 * GHOST)
    sources = jnp.where(is_live, jnp.where(from_ghost, ghost_source, own_source), 0)
    return (sources.reshape(N_GX, N_GY, EDGE_DEV), targets.reshape(N_GX, N_GY, EDGE_DEV))


def draw_edge_source(key, part):
    return edge_layout(key)[0]


def draw_edge_target(key, part):
    return edge_layout(key)[1]


def draw_send_list(key, part):
    base = jax.random.fold_in(key, 23)
    subkeys = jax.random.split(base, N_GX * N_GY * 8)

    def one_list(single):
        return jax.random.permutation(single, ATOM_DEV)[:GHOST]
    lists = jax.vmap(one_list)(subkeys)
    return lists.reshape(N_GX, N_GY, 8, GHOST)


def shard_levels(stream_key, shape, cuts, low, largest):
    def one(axis_at, blocks):
        draws = jax.random.uniform(jax.random.fold_in(jax.random.fold_in(stream_key, 6), axis_at), (blocks,), jnp.float32, low / len(cuts), largest / len(cuts))
        return jnp.repeat(jnp.exp(draws), shape[axis_at] // blocks).reshape((-1,) + (1,) * (len(shape) - axis_at - 1))

    loudness = one(*cuts[0])
    for cut in cuts[1:]:
        loudness = loudness * one(*cut)
    return loudness


def gaussian(key, extent, scale, reach, shards=(), held_as=jnp.bfloat16):
    result = jax.random.normal(key, extent, jnp.float32) * scale
    if len(shards) > 0:
        result = shard_levels(key, extent, shards, -0.22, 0.18) * result
    return jnp.clip(result, min=-reach, max=reach).astype(held_as)


def setup_inputs(seed: int = 0) -> dict:
    arg_keys = jax.random.split(jax.random.key(seed), 14)
    return {
        "features": gaussian(arg_keys[0], (N_GX, N_GY, 25 * CH, ATOM_DEV), 1.0, 6.0, ((0, 16), (1, 32))),
        "cotangent": gaussian(arg_keys[1], (N_GX, N_GY, 25 * CH, ATOM_DEV), 1.0, 6.0, ((0, 16), (1, 32))),
        "w_order0": gaussian(arg_keys[2], (5 * CH, 5 * CH), (5 * CH) ** -0.5, 0.3125),
        "w_order1": gaussian(arg_keys[3], (2, 4 * CH, 4 * CH), (4 * CH) ** -0.5, 0.375),
        "w_order2": gaussian(arg_keys[4], (2, 3 * CH, 3 * CH), (3 * CH) ** -0.5, 0.4375),
        "w_order3": gaussian(arg_keys[5], (2, 2 * CH, 2 * CH), (2 * CH) ** -0.5, 0.5),
        "w_order4": gaussian(arg_keys[6], (2, CH, CH), CH ** -0.5, 0.75),
        "to_grid": gaussian(arg_keys[7], (GRID, 25), 25 ** -0.5, 1.25, (), jnp.float32),
        "from_grid": gaussian(arg_keys[8], (25, GRID), GRID ** -0.5, 0.625, (), jnp.float32),
        "edge_harmonics": gaussian(arg_keys[9], (N_GX, N_GY, 25, EDGE_DEV), 1.0, 5.0, ((0, 16), (1, 32)), jnp.float32),
        "edge_source": draw_edge_source(jax.random.fold_in(arg_keys[13], 71), 0),
        "edge_target": draw_edge_target(jax.random.fold_in(arg_keys[13], 71), 0),
        "send_list": draw_send_list(jax.random.fold_in(arg_keys[13], 71), 0),
    }


DIRECTIONS = ((-1, -1), (-1, 0), (-1, 1), (0, -1), (0, 1), (1, -1), (1, 0), (1, 1))
edge_norm = 0.35


def order_spans(channels):
    spans = []
    offset = 5 * channels
    for degree_gap in range(1, 5):
        length = (5 - degree_gap) * channels
        spans.append((offset, offset + length, offset + 2 * length))
        offset = offset + 2 * length
    return spans


def mix_forward(filtered, weights, channels):
    zero_rows = 5 * channels
    pieces = [jnp.dot(weights[0], filtered[:zero_rows], preferred_element_type=jnp.float32)]
    for number, (begin_row, mid_row, end_row) in enumerate(order_spans(channels)):
        matrix = weights[number + 1]
        plus_rows = filtered[begin_row:mid_row]
        minus_rows = filtered[mid_row:end_row]
        pieces.append(jnp.dot(matrix[0], plus_rows, preferred_element_type=jnp.float32)
                      - jnp.dot(matrix[1], minus_rows, preferred_element_type=jnp.float32))
        pieces.append(jnp.dot(matrix[1], plus_rows, preferred_element_type=jnp.float32)
                      + jnp.dot(matrix[0], minus_rows, preferred_element_type=jnp.float32))
    return jnp.concatenate(pieces, axis=0)


def mix_backward(grads_in, weights, channels):
    zero_rows = 5 * channels
    pieces = [jnp.dot(weights[0].T, grads_in[:zero_rows], preferred_element_type=jnp.float32)]
    for number, (begin_row, mid_row, end_row) in enumerate(order_spans(channels)):
        matrix = weights[number + 1]
        plus_rows = grads_in[begin_row:mid_row]
        minus_rows = grads_in[mid_row:end_row]
        pieces.append(jnp.dot(matrix[0].T, plus_rows, preferred_element_type=jnp.float32)
                      + jnp.dot(matrix[1].T, minus_rows, preferred_element_type=jnp.float32))
        pieces.append(jnp.dot(matrix[0].T, minus_rows, preferred_element_type=jnp.float32)
                      - jnp.dot(matrix[1].T, plus_rows, preferred_element_type=jnp.float32))
    return jnp.concatenate(pieces, axis=0)


def apply_harmonics(columns, harmonics, channels):
    edge_count = columns.shape[1]
    shaped = columns.astype(jnp.float32).reshape(25, channels, edge_count)
    return (shaped * harmonics[:, None, :]).reshape(25 * channels, edge_count)


def edge_forward(extended, sources, targets, harmonics, weights, atoms, blocks_used):
    feature_rows = extended.shape[0]
    channels = feature_rows // 25

    def visit_block(block_id, running):
        row_begin = block_id * EDGE_BLOCK
        source_ids = lax.dynamic_slice_in_dim(sources, row_begin, EDGE_BLOCK)
        target_ids = lax.dynamic_slice_in_dim(targets, row_begin, EDGE_BLOCK)
        harmonic_block = lax.dynamic_slice_in_dim(harmonics, row_begin, EDGE_BLOCK, 1)
        columns = jnp.take(extended, source_ids, axis=1)
        filtered = apply_harmonics(columns, harmonic_block, channels).astype(jnp.bfloat16)
        message = mix_forward(filtered, weights, channels)
        return running.at[:, target_ids].add(message, mode="drop")

    start_sum = jnp.zeros((feature_rows, atoms), jnp.float32)
    return lax.fori_loop(0, blocks_used, visit_block, start_sum)


def edge_backward(d_aggregate, sources, targets, harmonics, weights, extended_cols, blocks_used):
    feature_rows = d_aggregate.shape[0]
    channels = feature_rows // 25

    def visit_block(block_id, running):
        row_begin = block_id * EDGE_BLOCK
        source_ids = lax.dynamic_slice_in_dim(sources, row_begin, EDGE_BLOCK)
        target_ids = lax.dynamic_slice_in_dim(targets, row_begin, EDGE_BLOCK)
        harmonic_block = lax.dynamic_slice_in_dim(harmonics, row_begin, EDGE_BLOCK, 1)
        grads_in = jnp.take(d_aggregate, target_ids, axis=1, mode="fill", fill_value=0)
        d_filtered = mix_backward(grads_in, weights, channels)
        d_source = apply_harmonics(d_filtered, harmonic_block, channels)
        return running.at[:, source_ids].add(d_source)

    start_sum = jnp.zeros((feature_rows, extended_cols), jnp.float32)
    return lax.fori_loop(0, blocks_used, visit_block, start_sum)


def node_forward(features, aggregate, to_grid, from_grid):
    channels = features.shape[0] // 25
    atoms = features.shape[1]
    scaled = (aggregate * edge_norm).reshape(25, channels, atoms)
    feature_f32 = features.astype(jnp.float32).reshape(25, channels, atoms)
    grid_agg = jnp.einsum("gk,kca->gca", to_grid, scaled, precision=lax.Precision.HIGHEST)
    grid_feat = jnp.einsum("gk,kca->gca", to_grid, feature_f32, precision=lax.Precision.HIGHEST)
    sigmoid_agg = jax.nn.sigmoid(grid_agg)
    activated = grid_agg * sigmoid_agg
    update = jnp.einsum("kg,gca->kca", from_grid, activated * grid_feat, precision=lax.Precision.HIGHEST)
    layer_out = (feature_f32 + update).reshape(25 * channels, atoms).astype(jnp.bfloat16)
    return layer_out, (grid_agg, grid_feat, sigmoid_agg, activated)


def node_backward(cotangent, saved, to_grid, from_grid):
    grid_agg, grid_feat, sigmoid_agg, activated = saved
    channels = cotangent.shape[0] // 25
    atoms = cotangent.shape[1]
    cot_f32 = cotangent.astype(jnp.float32).reshape(25, channels, atoms)
    d_product = jnp.einsum("kg,kca->gca", from_grid, cot_f32, precision=lax.Precision.HIGHEST)
    d_grid_agg = d_product * grid_feat * (sigmoid_agg * (1.0 + grid_agg * (1.0 - sigmoid_agg)))
    d_grid_feat = d_product * activated
    node_grad = cot_f32 + jnp.einsum("gk,gca->kca", to_grid, d_grid_feat, precision=lax.Precision.HIGHEST)
    d_aggregate = jnp.einsum("gk,gca->kca", to_grid, d_grid_agg, precision=lax.Precision.HIGHEST) * edge_norm
    d_aggregate = d_aggregate.reshape(25 * channels, atoms).astype(jnp.bfloat16)
    return node_grad.reshape(25 * channels, atoms), d_aggregate


def pick_columns(matrix, indices):
    return jnp.take(matrix, indices, axis=1)


def add_columns(matrix, indices, values):
    return matrix.at[:, indices].add(values)


def reference(features, cotangent, w_order0, w_order1, w_order2, w_order3, w_order4, to_grid, from_grid, edge_harmonics, edge_source, edge_target, send_list):
    weights = (w_order0, w_order1, w_order2, w_order3, w_order4)
    grid_x = features.shape[0]
    grid_y = features.shape[1]
    feature_rows = features.shape[2]
    atoms = features.shape[3]
    ghost_width = send_list.shape[3]
    ghost_blocks = []
    for index, (shift_x, shift_y) in enumerate(DIRECTIONS):
        moved_feat = jnp.roll(features, (-shift_x, -shift_y), axis=(0, 1))
        moved_list = jnp.roll(send_list[:, :, index], (-shift_x, -shift_y), axis=(0, 1))
        ghost_blocks.append(jax.vmap(jax.vmap(pick_columns))(moved_feat, moved_list))
    ghosts = jnp.concatenate(ghost_blocks, axis=3)

    def flatten_cells(array):
        return array.reshape((grid_x * grid_y,) + array.shape[2:])

    def per_cell(packed):
        own, ghost_cols, cot_cell, sources, targets, harmonics = packed
        extended = jnp.concatenate([own, ghost_cols], axis=1)
        live_count = jnp.sum((targets < atoms).astype(jnp.int32)).astype(jnp.int32)
        blocks_used = ((live_count + EDGE_BLOCK - 1) // EDGE_BLOCK).astype(jnp.int32)
        aggregate = edge_forward(extended, sources, targets, harmonics, weights, atoms, blocks_used)
        layer_cell, saved = node_forward(own, aggregate, to_grid, from_grid)
        node_grad, d_aggregate = node_backward(cot_cell, saved, to_grid, from_grid)
        d_extended = edge_backward(d_aggregate, sources, targets, harmonics, weights, extended.shape[1], blocks_used)
        return layer_cell, node_grad + d_extended[:, :atoms], d_extended[:, atoms:]

    packed_all = (flatten_cells(features), flatten_cells(ghosts), flatten_cells(cotangent),
                  flatten_cells(edge_source), flatten_cells(edge_target), flatten_cells(edge_harmonics))
    results = lax.map(per_cell, packed_all)
    layer_out = results[0].reshape(features.shape)
    local_grad = results[1].reshape(features.shape)
    ghost_grad = results[2].reshape(grid_x, grid_y, feature_rows, 8 * ghost_width)
    for index, (shift_x, shift_y) in enumerate(DIRECTIONS):
        piece = ghost_grad[:, :, :, index * ghost_width:(index + 1) * ghost_width]
        moved = jnp.roll(piece, (shift_x, shift_y), axis=(0, 1))
        local_grad = jax.vmap(jax.vmap(add_columns))(local_grad, send_list[:, :, index], moved)
    return layer_out, local_grad
```

```python
import functools

import jax
import jax.numpy as jnp
from jax import lax
from jax.experimental import pallas as pl
from jax.experimental.pallas import tpu as pltpu
from jax.sharding import PartitionSpec as P

DIRECTIONS = ((-1, -1), (-1, 0), (-1, 1), (0, -1), (0, 1), (1, -1), (1, 0), (1, 1))
EDGE_NORM = 0.35
MESH = pl.DeviceIdType.MESH
F32 = jnp.float32
BF16 = jnp.bfloat16

COEFS = 25
CH = 64
GRID = 100
ATOMS = 128
EDGES = 256
GHOST = 32
ROWS = COEFS * CH
GHOSTS = 8 * GHOST
SPANS = ((0, 320, 384), (320, 512, 512), (832, 384, 384), (1216, 256, 256), (1472, 128, 128))
ORDER = (1, 2, 0, 3, 4)
SEND_DIRS = (0, 2, 5, 7, 1, 6, 3, 4)


def nn(left, right):
    return jnp.dot(left, right, preferred_element_type=F32)


def nt(left, right):
    return lax.dot_general(left, right, (((1,), (1,)), ((), ())), preferred_element_type=F32)


def parts(value, count):
    pieces = []
    for _ in range(count - 1):
        piece = value.astype(BF16)
        pieces.append(piece)
        value = value - piece.astype(F32)
    pieces.append(value.astype(BF16))
    return pieces


def iota(shape, dim):
    return lax.broadcasted_iota(jnp.int32, shape, dim)


def ones_where(mask):
    return jnp.where(mask, 1.0, 0.0).astype(F32)


def identity(size):
    return ones_where(iota((size, size), 0) == iota((size, size), 1)).astype(BF16)


def kernel(
    count_x,
    count_y,
    feat_hbm,
    cot_hbm,
    w0_hbm,
    w1_hbm,
    w2_hbm,
    w3_hbm,
    w4_hbm,
    tg_hbm,
    fg_hbm,
    harm_hbm,
    source_ref,
    target_ref,
    list_ref,
    layer_ref,
    grad_ref,
    feat,
    cot,
    w0,
    w1,
    w2,
    w3,
    w4,
    tg,
    fg,
    harm,
    feat32,
    cot32,
    out0,
    out1,
    out2,
    out3,
    out4,
    in0,
    in1,
    in2,
    in3,
    in4,
    back0,
    back1,
    back2,
    back3,
    back4,
    home0,
    home1,
    home2,
    home3,
    home4,
    mix1,
    mix2,
    mix3,
    mix4,
    harm_t,
    pick_list,
    pick_source,
    pick_source_t,
    pick_target,
    pick_target_t,
    kron_a,
    kron_at,
    kron_b,
    kron_bt,
    grid_feat,
    d_product,
    product,
    d_feat,
    agg,
    d_agg,
    own_t,
    local_sem,
    out_sem,
    in_sem,
    back_sem,
    home_sem,
):
    outs = (out0, out1, out2, out3, out4)
    ins = (in0, in1, in2, in3, in4)
    backs = (back0, back1, back2, back3, back4)
    homes = (home0, home1, home2, home3, home4)
    mixes = (w0, mix1, mix2, mix3, mix4)

    at_x = lax.axis_index("gx")
    at_y = lax.axis_index("gy")

    def cell(index, sign):
        step_x, step_y = DIRECTIONS[index]
        return (
            lax.rem(at_x + (sign * step_x + count_x), count_x),
            lax.rem(at_y + (sign * step_y + count_y), count_y),
        )

    loads = [
        pltpu.make_async_copy(source, target, local_sem.at[number])
        for number, (source, target) in enumerate(
            (
                (feat_hbm, feat),
                (harm_hbm, harm),
                (tg_hbm, tg),
                (fg_hbm, fg),
                (cot_hbm, cot),
                (w0_hbm, w0),
                (w1_hbm, w1),
                (w2_hbm, w2),
                (w3_hbm, w3),
                (w4_hbm, w4),
            )
        )
    ]
    for load in loads:
        load.start()

    barrier = pltpu.get_barrier_semaphore()
    for index in range(8):
        pl.semaphore_signal(barrier, inc=1, device_id=cell(index, 1), device_id_type=MESH)

    list_row = nn(
        list_ref[...].astype(F32).astype(BF16),
        ones_where(iota((GHOST, GHOSTS), 0) == (iota((GHOST, GHOSTS), 1) & 31)).astype(BF16),
    )
    list_row = jnp.where(iota((8, GHOSTS), 0) == (iota((8, GHOSTS), 1) >> 5), list_row, 0.0)
    list_row = jnp.sum(list_row, axis=0, keepdims=True)
    pick_list[...] = ones_where(iota((ATOMS, GHOSTS), 0).astype(F32) == list_row).astype(BF16)
    eye = identity(256)
    pick_list_t = nt(eye, pick_list[...]).astype(BF16)

    loads[0].wait()

    lending = {}
    returning = {}
    started = False
    for order in ORDER:
        first, rows, lanes = SPANS[order]
        lent = nt(pick_list_t, feat[first : first + rows, :]).astype(BF16)
        outs[order][:, :, 0:rows] = lent.reshape(8, GHOST, rows)
        if not started:
            pl.semaphore_wait(barrier, 8)
            started = True
        for index in SEND_DIRS:
            copy = pltpu.make_async_remote_copy(
                src_ref=outs[order].at[index],
                dst_ref=ins[order].at[index],
                send_sem=out_sem.at[order, index],
                recv_sem=in_sem.at[order, index],
                device_id=cell(index, -1),
                device_id_type=MESH,
            )
            copy.start()
            lending[order, index] = copy

    pick_source[...] = ones_where(
        iota((ATOMS + GHOSTS, EDGES), 0) == source_ref[...]
    ).astype(BF16)
    pick_target[...] = ones_where(iota((ATOMS, EDGES), 0) == target_ref[...]).astype(BF16)
    pick_source_t[...] = nt(eye, pick_source[...]).astype(BF16)
    pick_target_t[...] = nt(eye, pick_target[...]).astype(BF16)

    loads[1].wait()
    harm_parts = [nt(eye, piece).astype(BF16) for piece in parts(harm[...], 3)]
    for order in ORDER:
        first, rows, lanes = SPANS[order]
        spread = ones_where(
            ((iota((COEFS, rows), 1) + first) >> 6) == iota((COEFS, rows), 0)
        ).astype(BF16)
        wide = nn(harm_parts[0], spread) + nn(harm_parts[1], spread) + nn(harm_parts[2], spread)
        harm_t[:, first : first + rows] = wide

    loads[2].wait()
    loads[3].wait()
    grid_rows = ones_where((iota((GRID * 8, GRID), 0) >> 3) == iota((GRID * 8, GRID), 1)).astype(BF16)
    grid_cols = ones_where((iota((GRID, GRID * 8), 1) >> 3) == iota((GRID, GRID * 8), 0)).astype(BF16)
    coef_rows = ones_where((iota((COEFS * 8, COEFS), 0) >> 3) == iota((COEFS * 8, COEFS), 1)).astype(BF16)
    coef_cols = ones_where((iota((COEFS, COEFS * 8), 1) >> 3) == iota((COEFS, COEFS * 8), 0)).astype(BF16)
    tall = (iota((GRID * 8, COEFS * 8), 0) & 7) == (iota((GRID * 8, COEFS * 8), 1) & 7)
    flat = (iota((COEFS * 8, GRID * 8), 0) & 7) == (iota((COEFS * 8, GRID * 8), 1) & 7)
    for number, (to_part, from_part) in enumerate(zip(parts(tg[...], 2), parts(fg[...], 2))):
        kron_a[number] = jnp.where(
            tall, nn(nn(grid_rows, to_part).astype(BF16), coef_cols), 0.0
        ).astype(BF16)
        kron_at[number] = jnp.where(
            flat, nn(nt(coef_rows, to_part).astype(BF16), grid_cols), 0.0
        ).astype(BF16)
        kron_b[number] = jnp.where(
            flat, nn(nn(coef_rows, from_part).astype(BF16), grid_cols), 0.0
        ).astype(BF16)
        kron_bt[number] = jnp.where(
            tall, nn(nt(grid_rows, from_part).astype(BF16), coef_cols), 0.0
        ).astype(BF16)

    feat32[...] = feat[...].astype(F32).reshape(COEFS, 8, 8, ATOMS)
    loads[4].wait()
    cot32[...] = cot[...].astype(F32).reshape(COEFS, 8, 8, ATOMS)

    def pair(ref, at):
        return jnp.concatenate(
            [ref[:, 2 * at + side].reshape(COEFS * 8, ATOMS) for side in range(2)], axis=1
        )

    def unpair(ref, at, value):
        for side in range(2):
            ref[:, 2 * at + side] = value[:, side * ATOMS : (side + 1) * ATOMS].reshape(
                COEFS, 8, ATOMS
            )

    def times(kron, value):
        high, low = parts(value, 2)
        return nn(kron[0], high) + nn(kron[1], high) + nn(kron[0], low)

    @pl.loop(0, 4)
    def _(at):
        feat_pair = pair(feat32, at).astype(BF16)
        grid_feat[at] = nn(kron_a[0], feat_pair) + nn(kron_a[1], feat_pair)
        cot_pair = pair(cot32, at).astype(BF16)
        d_product[at] = nn(kron_bt[0], cot_pair) + nn(kron_bt[1], cot_pair)

    for number in range(5, 10):
        loads[number].wait()
    for weight, mix in ((w1, mix1), (w2, mix2), (w3, mix3), (w4, mix4)):
        size = weight.shape[1]
        left = ones_where(iota((size, 2 * size), 0) == iota((size, 2 * size), 1)).astype(BF16)
        right = ones_where(iota((size, 2 * size), 0) + size == iota((size, 2 * size), 1)).astype(BF16)
        mix[0:size, :] = (nn(weight[0], left) - nn(weight[1], right)).astype(BF16)
        mix[size : 2 * size, :] = (nn(weight[1], left) + nn(weight[0], right)).astype(BF16)

    for order in ORDER:
        first, rows, lanes = SPANS[order]
        columns = nt(pick_source_t[:, 0:ATOMS], feat[first : first + rows, :])
        for index in SEND_DIRS:
            lending[order, index].wait_recv()
        ghosts = ins[order][...].reshape(GHOSTS, lanes)[:, 0:rows]
        columns = columns + nn(pick_source_t[:, ATOMS:], ghosts)
        filtered = (columns * harm_t[:, first : first + rows]).astype(BF16)
        message = nt(mixes[order][...], filtered)
        high, low = parts(message, 2)
        total = nt(high, pick_target[...]) + nt(low, pick_target[...])
        agg[first // CH : (first + rows) // CH] = (total * EDGE_NORM).reshape(
            rows // CH, 8, 8, ATOMS
        )

    @pl.loop(0, 4)
    def _(at):
        grid_agg = times(kron_a, pair(agg, at))
        gate = jax.nn.sigmoid(grid_agg)
        active = grid_agg * gate
        slope = gate * (1.0 + grid_agg * (1.0 - gate))
        feat_at = grid_feat[at]
        d_at = d_product[at]
        product[at] = active * feat_at
        d_feat[at] = d_at * active
        unpair(d_agg, at, times(kron_at, d_at * feat_at * slope) * EDGE_NORM)

    for order in ORDER:
        first, rows, lanes = SPANS[order]
        d_rows = d_agg[first // CH : (first + rows) // CH].reshape(rows, ATOMS).astype(BF16)
        d_message = nt(pick_target_t[...], d_rows).astype(BF16)
        d_filtered = nn(d_message, mixes[order][...])
        high, low = parts(d_filtered * harm_t[:, first : first + rows], 2)
        ghosts = nn(pick_source[ATOMS:, :], high) + nn(pick_source[ATOMS:, :], low)
        backs[order][:, :, 0:rows] = ghosts.astype(BF16).reshape(8, GHOST, rows)
        for index in SEND_DIRS:
            copy = pltpu.make_async_remote_copy(
                src_ref=backs[order].at[index],
                dst_ref=homes[order].at[index],
                send_sem=back_sem.at[order, index],
                recv_sem=home_sem.at[order, index],
                device_id=cell(index, 1),
                device_id_type=MESH,
            )
            copy.start()
            returning[order, index] = copy
        own_t[:, first : first + rows] = nn(pick_source[0:ATOMS, :], high) + nn(
            pick_source[0:ATOMS, :], low
        )

    @pl.loop(0, 4)
    def _(at):
        unpair(feat32, at, pair(feat32, at) + times(kron_b, product[at]))
        unpair(cot32, at, pair(cot32, at) + times(kron_at, d_feat[at]))

    layer_ref[...] = feat32[...].reshape(ROWS, ATOMS).astype(BF16)

    for order in ORDER:
        first, rows, lanes = SPANS[order]
        for index in SEND_DIRS:
            returning[order, index].wait_recv()
        arrived = homes[order][...].reshape(GHOSTS, lanes)[:, 0:rows]
        total = own_t[:, first : first + rows] + nn(pick_list[...], arrived)
        node = cot32[first // CH : (first + rows) // CH].reshape(rows, ATOMS)
        grad_ref[first : first + rows, :] = node + jnp.transpose(total)

    for copy in (*lending.values(), *returning.values()):
        copy.wait_send()


def per_device(
    features,
    cotangent,
    w_order0,
    w_order1,
    w_order2,
    w_order3,
    w_order4,
    to_grid,
    from_grid,
    edge_harmonics,
    edge_source,
    edge_target,
    send_list,
):
    count_x = lax.axis_size("gx")
    count_y = lax.axis_size("gy")
    in_hbm = pl.BlockSpec(memory_space=pl.ANY)
    in_vmem = pl.BlockSpec(memory_space=pltpu.VMEM)
    grids = pltpu.VMEM((4, GRID * 8, 2 * ATOMS), F32)
    tiles = pltpu.VMEM((COEFS, 8, 8, ATOMS), F32)
    tall = pltpu.VMEM((2, GRID * 8, COEFS * 8), BF16)
    flat = pltpu.VMEM((2, COEFS * 8, GRID * 8), BF16)
    blocks = [pltpu.VMEM((8, GHOST, lanes), BF16) for _, _, lanes in SPANS]
    copies = pltpu.SemaphoreType.DMA((5, 8))
    layer, grad = pl.pallas_call(
        functools.partial(kernel, count_x, count_y),
        out_shape=(
            jax.ShapeDtypeStruct((ROWS, ATOMS), BF16),
            jax.ShapeDtypeStruct((ROWS, ATOMS), F32),
        ),
        in_specs=[in_hbm] * 10 + [in_vmem] * 3,
        out_specs=(in_vmem, in_vmem),
        scratch_shapes=[
            pltpu.VMEM((ROWS, ATOMS), BF16),
            pltpu.VMEM((ROWS, ATOMS), BF16),
            pltpu.VMEM(w_order0.shape, BF16),
            pltpu.VMEM(w_order1.shape, BF16),
            pltpu.VMEM(w_order2.shape, BF16),
            pltpu.VMEM(w_order3.shape, BF16),
            pltpu.VMEM(w_order4.shape, BF16),
            pltpu.VMEM((GRID, COEFS), F32),
            pltpu.VMEM((COEFS, GRID), F32),
            pltpu.VMEM((COEFS, EDGES), F32),
            tiles,
            tiles,
            *blocks,
            *blocks,
            *blocks,
            *blocks,
            *[pltpu.VMEM((rows, rows), BF16) for _, rows, _ in SPANS[1:]],
            pltpu.VMEM((EDGES, ROWS), F32),
            pltpu.VMEM((ATOMS, GHOSTS), BF16),
            pltpu.VMEM((ATOMS + GHOSTS, EDGES), BF16),
            pltpu.VMEM((EDGES, ATOMS + GHOSTS), BF16),
            pltpu.VMEM((ATOMS, EDGES), BF16),
            pltpu.VMEM((EDGES, ATOMS), BF16),
            tall,
            flat,
            flat,
            tall,
            grids,
            grids,
            grids,
            grids,
            tiles,
            tiles,
            pltpu.VMEM((ATOMS, ROWS), F32),
            pltpu.SemaphoreType.DMA((10,)),
            copies,
            copies,
            copies,
            copies,
        ],
        compiler_params=pltpu.CompilerParams(
            collective_id=0, has_side_effects=True, vmem_limit_bytes=56 * 1024 * 1024
        ),
        name="layer",
    )(
        features[0, 0],
        cotangent[0, 0],
        w_order0,
        w_order1,
        w_order2,
        w_order3,
        w_order4,
        to_grid,
        from_grid,
        edge_harmonics[0, 0],
        edge_source[0],
        edge_target[0],
        send_list[0, 0],
    )
    return layer[None, None], grad[None, None]


def solution(mesh):
    cells = P("gx", "gy", None, None)
    placed = (cells, cells, P(), P(), P(), P(), P(), P(), P(), cells, P("gx", "gy", None), P("gx", "gy", None), cells)
    return jax.shard_map(
        per_device,
        mesh=mesh,
        in_specs=placed,
        out_specs=(cells, cells),
        check_vma=False,
    )
```

```python
import functools

import jax
import jax.numpy as jnp
from jax import lax
from jax.experimental import pallas as pl
from jax.experimental.pallas import tpu as pltpu
from jax.sharding import PartitionSpec as P

DIRECTIONS = ((-1, -1), (-1, 0), (-1, 1), (0, -1), (0, 1), (1, -1), (1, 0), (1, 1))
EDGE_NORM = 0.35
MESH = pl.DeviceIdType.MESH
F32 = jnp.float32
BF16 = jnp.bfloat16

COEFS = 25
CH = 64
GRID = 100
ATOMS = 128
EDGES = 256
GHOST = 32
ROWS = COEFS * CH
GHOSTS = 8 * GHOST
SPANS = ((0, 320, 384), (320, 512, 512), (832, 384, 384), (1216, 256, 256), (1472, 128, 128))
ORDER = (3, 0, 1, 2, 4)
BACK_ORDER = (4, 0, 1, 2, 3)
STRIPES = ((0, 256), (256, 256), (512, 256), (768, 32))
SEND_DIRS = (0, 2, 5, 7, 1, 6, 3, 4)


def nn(left, right):
    return jnp.dot(left, right, preferred_element_type=F32)


def nt(left, right):
    return lax.dot_general(left, right, (((1,), (1,)), ((), ())), preferred_element_type=F32)


def parts(value, count):
    pieces = []
    for _ in range(count - 1):
        piece = value.astype(BF16)
        pieces.append(piece)
        value = value - piece.astype(F32)
    pieces.append(value.astype(BF16))
    return pieces


def iota(shape, dim):
    return lax.broadcasted_iota(jnp.int32, shape, dim)


def ones_where(mask):
    return jnp.where(mask, 1.0, 0.0).astype(F32)


def identity(size):
    return ones_where(iota((size, size), 0) == iota((size, size), 1)).astype(BF16)


def kernel(
    count_x,
    count_y,
    feat_hbm,
    cot_hbm,
    w0_hbm,
    w1_hbm,
    w2_hbm,
    w3_hbm,
    w4_hbm,
    tg_hbm,
    fg_hbm,
    harm_hbm,
    source_hbm,
    target_hbm,
    list_hbm,
    layer_ref,
    grad_ref,
    feat,
    cot,
    w0,
    w1,
    w2,
    w3,
    w4,
    tg,
    fg,
    harm,
    source_ref,
    target_ref,
    list_ref,
    feat32,
    cot32,
    out0,
    out1,
    out2,
    out3,
    out4,
    in0,
    in1,
    in2,
    in3,
    in4,
    back0,
    back1,
    back2,
    back3,
    back4,
    home0,
    home1,
    home2,
    home3,
    home4,
    mix1,
    mix2,
    mix3,
    mix4,
    harm_t,
    pick_list,
    pick_source,
    pick_source_t,
    pick_target,
    pick_target_t,
    kron_a,
    kron_at,
    kron_b,
    kron_bt,
    grid_feat,
    d_product,
    grid_agg,
    joint,
    agg,
    d_agg,
    own_t,
    local_sem,
    out_sem,
    in_sem,
    back_sem,
    home_sem,
):
    outs = (out0, out1, out2, out3, out4)
    ins = (in0, in1, in2, in3, in4)
    backs = (back0, back1, back2, back3, back4)
    homes = (home0, home1, home2, home3, home4)
    mixes = (w0, mix1, mix2, mix3, mix4)

    at_x = lax.axis_index("gx")
    at_y = lax.axis_index("gy")

    def cell(index, sign):
        step_x, step_y = DIRECTIONS[index]
        return (
            lax.rem(at_x + (sign * step_x + count_x), count_x),
            lax.rem(at_y + (sign * step_y + count_y), count_y),
        )

    loads = [
        pltpu.make_async_copy(source, target, local_sem.at[number])
        for number, (source, target) in enumerate(
            (
                (list_hbm, list_ref),
                (feat_hbm, feat),
                (source_hbm, source_ref),
                (target_hbm, target_ref),
                (harm_hbm.at[:, 0], harm),
                (tg_hbm, tg),
                (fg_hbm, fg),
                (cot_hbm, cot),
                (w0_hbm, w0),
                (w1_hbm, w1),
                (w2_hbm, w2),
                (w3_hbm, w3),
                (w4_hbm, w4),
            )
        )
    ]
    for load in loads:
        load.start()

    barrier = pltpu.get_barrier_semaphore()
    for index in range(8):
        pl.semaphore_signal(barrier, inc=1, device_id=cell(index, 1), device_id_type=MESH)

    loads[0].wait()
    list_row = nn(
        list_ref[...].astype(F32).astype(BF16),
        ones_where(iota((GHOST, GHOSTS), 0) == (iota((GHOST, GHOSTS), 1) & 31)).astype(BF16),
    )
    list_row = jnp.where(iota((8, GHOSTS), 0) == (iota((8, GHOSTS), 1) >> 5), list_row, 0.0)
    list_row = jnp.sum(list_row, axis=0, keepdims=True)
    pick_list[...] = ones_where(iota((ATOMS, GHOSTS), 0).astype(F32) == list_row).astype(BF16)
    eye = identity(256)
    pick_list_t = nt(eye, pick_list[...]).astype(BF16)

    loads[1].wait()

    lending = {}
    returning = {}
    started = False
    for order in ORDER:
        first, rows, lanes = SPANS[order]
        lent = nt(pick_list_t, feat[first : first + rows, :]).astype(BF16)
        outs[order][:, :, 0:rows] = lent.reshape(8, GHOST, rows)
        if not started:
            pl.semaphore_wait(barrier, 8)
            started = True
        for index in SEND_DIRS:
            copy = pltpu.make_async_remote_copy(
                src_ref=outs[order].at[index],
                dst_ref=ins[order].at[index],
                send_sem=out_sem.at[order, index],
                recv_sem=in_sem.at[order, index],
                device_id=cell(index, -1),
                device_id_type=MESH,
            )
            copy.start()
            lending[order, index] = copy

    loads[2].wait()
    loads[3].wait()
    pick_source[...] = ones_where(
        iota((ATOMS + GHOSTS, EDGES), 0) == source_ref[...]
    ).astype(BF16)
    pick_target[...] = ones_where(iota((ATOMS, EDGES), 0) == target_ref[...]).astype(BF16)
    pick_source_t[...] = nt(eye, pick_source[...]).astype(BF16)
    pick_target_t[...] = nt(eye, pick_target[...]).astype(BF16)

    loads[4].wait()
    harm_parts = [nt(eye, piece).astype(BF16) for piece in parts(harm[...], 3)]
    for order in ORDER:
        first, rows, lanes = SPANS[order]
        spread = ones_where(
            ((iota((COEFS, rows), 1) + first) >> 6) == iota((COEFS, rows), 0)
        ).astype(BF16)
        wide = nn(harm_parts[0], spread) + nn(harm_parts[1], spread) + nn(harm_parts[2], spread)
        harm_t[:, first : first + rows] = wide

    loads[5].wait()
    loads[6].wait()
    grid_rows = ones_where((iota((GRID * 8, GRID), 0) >> 3) == iota((GRID * 8, GRID), 1)).astype(BF16)
    grid_cols = ones_where((iota((GRID, GRID * 8), 1) >> 3) == iota((GRID, GRID * 8), 0)).astype(BF16)
    coef_rows = ones_where((iota((COEFS * 8, COEFS), 0) >> 3) == iota((COEFS * 8, COEFS), 1)).astype(BF16)
    coef_cols = ones_where((iota((COEFS, COEFS * 8), 1) >> 3) == iota((COEFS, COEFS * 8), 0)).astype(BF16)
    tall = (iota((GRID * 8, COEFS * 8), 0) & 7) == (iota((GRID * 8, COEFS * 8), 1) & 7)
    flat = (iota((COEFS * 8, GRID * 8), 0) & 7) == (iota((COEFS * 8, GRID * 8), 1) & 7)
    for number, (to_part, from_part) in enumerate(zip(parts(tg[...], 2), parts(fg[...], 2))):
        kron_a[number] = jnp.where(
            tall, nn(nt(grid_rows, to_part).astype(BF16), coef_cols), 0.0
        ).astype(BF16)
        kron_at[number] = jnp.where(
            flat, nn(nn(coef_rows, to_part).astype(BF16), grid_cols), 0.0
        ).astype(BF16)
        kron_b[number] = jnp.where(
            flat, nn(nn(coef_rows, from_part).astype(BF16), grid_cols), 0.0
        ).astype(BF16)
        kron_bt[number] = jnp.where(
            tall, nn(nt(grid_rows, from_part).astype(BF16), coef_cols), 0.0
        ).astype(BF16)

    feat32[...] = feat[...].astype(F32).reshape(COEFS, 8, 8, ATOMS)
    loads[7].wait()
    cot32[...] = cot[...].astype(F32).reshape(COEFS, 8, 8, ATOMS)

    def pair(ref, at):
        return jnp.concatenate(
            [ref[:, 2 * at + side].reshape(COEFS * 8, ATOMS) for side in range(2)], axis=1
        )

    def unpair(ref, at, value):
        for side in range(2):
            ref[:, 2 * at + side] = value[:, side * ATOMS : (side + 1) * ATOMS].reshape(
                COEFS, 8, ATOMS
            )

    def times(kron, value, stripe):
        high, low = parts(value, 2)
        return (
            nn(kron[0, :, stripe], high) + nn(kron[1, :, stripe], high) + nn(kron[0, :, stripe], low)
        )

    @pl.loop(0, 4)
    def _(at):
        feat_pair = pair(feat32, at).astype(BF16)
        grid_feat[at] = nn(kron_a[0], feat_pair) + nn(kron_a[1], feat_pair)
        cot_pair = pair(cot32, at).astype(BF16)
        d_product[at] = nn(kron_bt[0], cot_pair) + nn(kron_bt[1], cot_pair)
        joint[at] = grid_feat[at] * d_product[at]

    for number in range(8, 13):
        loads[number].wait()
    for weight, mix in ((w1, mix1), (w2, mix2), (w3, mix3), (w4, mix4)):
        size = weight.shape[1]
        left = ones_where(iota((size, 2 * size), 0) == iota((size, 2 * size), 1)).astype(BF16)
        right = ones_where(iota((size, 2 * size), 0) + size == iota((size, 2 * size), 1)).astype(BF16)
        mix[0:size, :] = (nn(weight[0], left) - nn(weight[1], right)).astype(BF16)
        mix[size : 2 * size, :] = (nn(weight[1], left) + nn(weight[0], right)).astype(BF16)

    for order in ORDER:
        first, rows, lanes = SPANS[order]
        columns = nt(pick_source_t[:, 0:ATOMS], feat[first : first + rows, :])
        for index in SEND_DIRS:
            lending[order, index].wait_recv()
        ghosts = ins[order][...].reshape(GHOSTS, lanes)[:, 0:rows]
        columns = columns + nn(pick_source_t[:, ATOMS:], ghosts)
        filtered = (columns * harm_t[:, first : first + rows]).astype(BF16)
        message = nt(mixes[order][...], filtered)
        high, low = parts(message, 2)
        total = nt(high, pick_target[...]) + nt(low, pick_target[...])
        agg[first // CH : (first + rows) // CH] = (total * EDGE_NORM).reshape(
            rows // CH, 8, 8, ATOMS
        )

    @pl.loop(0, 4)
    def _(at):
        agg_pair = pair(agg, at).astype(BF16)
        total = None
        for begin, size in STRIPES:
            stripe = slice(begin, begin + size)
            rough = nn(kron_a[0, stripe, :], agg_pair)
            grid_agg[at, stripe, :] = rough
            gate = 0.5 + 0.5 * jnp.tanh(0.5 * rough)
            slope = gate * (1.0 + rough * (1.0 - gate))
            term = nn(kron_at[0, :, stripe], (joint[at, stripe, :] * slope).astype(BF16))
            total = term if total is None else total + term
        unpair(d_agg, at, total * EDGE_NORM)

    for order in BACK_ORDER:
        first, rows, lanes = SPANS[order]
        d_rows = d_agg[first // CH : (first + rows) // CH].reshape(rows, ATOMS).astype(BF16)
        d_message = nt(pick_target_t[...], d_rows).astype(BF16)
        d_filtered = nn(d_message, mixes[order][...])
        high, low = parts(d_filtered * harm_t[:, first : first + rows], 2)
        ghosts = nn(pick_source[ATOMS:, :], high)
        backs[order][:, :, 0:rows] = ghosts.astype(BF16).reshape(8, GHOST, rows)
        for index in SEND_DIRS:
            copy = pltpu.make_async_remote_copy(
                src_ref=backs[order].at[index],
                dst_ref=homes[order].at[index],
                send_sem=back_sem.at[order, index],
                recv_sem=home_sem.at[order, index],
                device_id=cell(index, 1),
                device_id_type=MESH,
            )
            copy.start()
            returning[order, index] = copy
        own_t[:, first : first + rows] = nn(pick_source[0:ATOMS, :], high) + nn(
            pick_source[0:ATOMS, :], low
        )

    @pl.loop(0, 4)
    def _(at):
        agg_high, agg_low = parts(pair(agg, at), 2)
        update = None
        for begin, size in STRIPES:
            stripe = slice(begin, begin + size)
            exact = (
                grid_agg[at, stripe, :]
                + nn(kron_a[1, stripe, :], agg_high)
                + nn(kron_a[0, stripe, :], agg_low)
            )
            active = exact * jax.nn.sigmoid(exact)
            made = times(kron_b, active * grid_feat[at, stripe, :], stripe)
            back = times(kron_at, active * d_product[at, stripe, :], stripe)
            update = made if update is None else update + made
            d_node = back if begin == 0 else d_node + back
        unpair(feat32, at, pair(feat32, at) + update)
        unpair(cot32, at, pair(cot32, at) + d_node)

    layer_ref[...] = feat32[...].reshape(ROWS, ATOMS).astype(BF16)

    for order in BACK_ORDER:
        first, rows, lanes = SPANS[order]
        for index in SEND_DIRS:
            returning[order, index].wait_recv()
        arrived = homes[order][...].reshape(GHOSTS, lanes)[:, 0:rows]
        total = own_t[:, first : first + rows] + nn(pick_list[...], arrived)
        node = cot32[first // CH : (first + rows) // CH].reshape(rows, ATOMS)
        grad_ref[first : first + rows, :] = node + jnp.transpose(total)

    for copy in (*lending.values(), *returning.values()):
        copy.wait_send()


def per_device(
    features,
    cotangent,
    w_order0,
    w_order1,
    w_order2,
    w_order3,
    w_order4,
    to_grid,
    from_grid,
    edge_harmonics,
    edge_source,
    edge_target,
    send_list,
):
    count_x = lax.axis_size("gx")
    count_y = lax.axis_size("gy")
    in_hbm = pl.BlockSpec(memory_space=pltpu.HBM)
    vmem = pl.BlockSpec(memory_space=pltpu.VMEM)
    grids = pltpu.VMEM((4, GRID * 8, 2 * ATOMS), F32)
    tiles = pltpu.VMEM((COEFS, 8, 8, ATOMS), F32)
    tall = pltpu.VMEM((2, GRID * 8, COEFS * 8), BF16)
    flat = pltpu.VMEM((2, COEFS * 8, GRID * 8), BF16)
    blocks = [pltpu.VMEM((8, GHOST, lanes), BF16) for _, _, lanes in SPANS]
    copies = pltpu.SemaphoreType.DMA((5, 8))
    layer, grad = pl.pallas_call(
        functools.partial(kernel, count_x, count_y),
        out_shape=(
            jax.ShapeDtypeStruct((ROWS, ATOMS), BF16),
            jax.ShapeDtypeStruct((ROWS, ATOMS), F32),
        ),
        in_specs=[in_hbm] * 13,
        out_specs=(vmem, vmem),
        scratch_shapes=[
            pltpu.VMEM((ROWS, ATOMS), BF16),
            pltpu.VMEM((ROWS, ATOMS), BF16),
            pltpu.VMEM(w_order0.shape, BF16),
            pltpu.VMEM(w_order1.shape, BF16),
            pltpu.VMEM(w_order2.shape, BF16),
            pltpu.VMEM(w_order3.shape, BF16),
            pltpu.VMEM(w_order4.shape, BF16),
            pltpu.VMEM((COEFS, GRID), F32),
            pltpu.VMEM((COEFS, GRID), F32),
            pltpu.VMEM((COEFS, EDGES), F32),
            pltpu.VMEM((1, EDGES), jnp.int32),
            pltpu.VMEM((1, EDGES), jnp.int32),
            pltpu.VMEM((8, GHOST), jnp.int32),
            tiles,
            tiles,
            *blocks,
            *blocks,
            *blocks,
            *blocks,
            *[pltpu.VMEM((rows, rows), BF16) for _, rows, _ in SPANS[1:]],
            pltpu.VMEM((EDGES, ROWS), F32),
            pltpu.VMEM((ATOMS, GHOSTS), BF16),
            pltpu.VMEM((ATOMS + GHOSTS, EDGES), BF16),
            pltpu.VMEM((EDGES, ATOMS + GHOSTS), BF16),
            pltpu.VMEM((ATOMS, EDGES), BF16),
            pltpu.VMEM((EDGES, ATOMS), BF16),
            tall,
            flat,
            flat,
            tall,
            grids,
            grids,
            grids,
            grids,
            tiles,
            tiles,
            pltpu.VMEM((ATOMS, ROWS), F32),
            pltpu.SemaphoreType.DMA((13,)),
            copies,
            copies,
            copies,
            copies,
        ],
        compiler_params=pltpu.CompilerParams(
            collective_id=0, has_side_effects=True, vmem_limit_bytes=40 * 1024 * 1024
        ),
        name="layer",
    )(
        *[
            pltpu.with_memory_space_constraint(value, pltpu.HBM)
            for value in (
                features[0, 0],
                cotangent[0, 0],
                w_order0,
                w_order1,
                w_order2,
                w_order3,
                w_order4,
                to_grid.T,
                from_grid,
                edge_harmonics[0, 0].reshape(COEFS, 1, EDGES),
                edge_source[0],
                edge_target[0],
                send_list[0, 0],
            )
        ],
    )
    return layer[None, None], grad[None, None]


def solution(mesh):
    cells = P("gx", "gy", None, None)
    placed = (cells, cells, P(), P(), P(), P(), P(), P(), P(), cells, P("gx", "gy", None), P("gx", "gy", None), cells)
    return jax.shard_map(
        per_device,
        mesh=mesh,
        in_specs=placed,
        out_specs=(cells, cells),
        check_vma=False,
    )
```

```python
import functools

import jax
import jax.numpy as jnp
from jax import lax
from jax.experimental import pallas as pl
from jax.experimental.pallas import tpu as pltpu
from jax.sharding import PartitionSpec as P

DIRECTIONS = ((-1, -1), (-1, 0), (-1, 1), (0, -1), (0, 1), (1, -1), (1, 0), (1, 1))
EDGE_NORM = 0.35
MESH = pl.DeviceIdType.MESH
F32 = jnp.float32
BF16 = jnp.bfloat16

COEFS = 25
CH = 64
GRID = 100
ATOMS = 128
EDGES = 256
GHOST = 32
ROWS = COEFS * CH
GHOSTS = 8 * GHOST
SPANS = ((0, 320, 256), (320, 512, 512), (832, 384, 384), (1216, 256, 256), (1472, 128, 128))
ORDER = (3, 0, 1, 2, 4)
BACK_ORDER = (4, 0, 1, 2, 3)
STRIPES = ((0, 256), (256, 256), (512, 256), (768, 32))
SEND_DIRS = (0, 2, 5, 7, 1, 6, 3, 4)
LEND_FIRST = (0, 2, 1)
LEND_REST = (5, 7, 6, 3, 4)
RETURN_FIRST = (5, 7, 6)
RETURN_REST = (0, 2, 1, 3, 4)


def nn(left, right):
    return jnp.dot(left, right, preferred_element_type=F32)


def nt(left, right):
    return lax.dot_general(left, right, (((1,), (1,)), ((), ())), preferred_element_type=F32)


def parts(value, count):
    pieces = []
    for _ in range(count - 1):
        piece = value.astype(BF16)
        pieces.append(piece)
        value = value - piece.astype(F32)
    pieces.append(value.astype(BF16))
    return pieces


def iota(shape, dim):
    return lax.broadcasted_iota(jnp.int32, shape, dim)


def ones_where(mask):
    return jnp.where(mask, 1.0, 0.0).astype(F32)


def identity(size):
    return ones_where(iota((size, size), 0) == iota((size, size), 1)).astype(BF16)


def kernel(
    count_x,
    count_y,
    feat_hbm,
    cot_hbm,
    w0_hbm,
    w1_hbm,
    w2_hbm,
    w3_hbm,
    w4_hbm,
    tg_hbm,
    fg_hbm,
    harm_hbm,
    source_hbm,
    target_hbm,
    list_hbm,
    layer_ref,
    grad_ref,
    feat,
    cot,
    w0,
    w1,
    w2,
    w3,
    w4,
    tg,
    fg,
    harm,
    source_ref,
    target_ref,
    list_ref,
    feat32,
    cot32,
    out0,
    out1,
    out2,
    out3,
    out4,
    out5,
    in0,
    in1,
    in2,
    in3,
    in4,
    in5,
    back0,
    back1,
    back2,
    back3,
    back4,
    back5,
    home0,
    home1,
    home2,
    home3,
    home4,
    home5,
    mix1,
    mix2,
    mix3,
    mix4,
    harm_t,
    pick_list,
    pick_source,
    pick_source_t,
    pick_target,
    pick_target_t,
    kron_a,
    kron_at,
    kron_b,
    kron_bt,
    grid_feat,
    d_product,
    grid_agg,
    joint,
    agg,
    d_agg,
    own_t,
    local_sem,
    feat_sem,
    out_sem,
    in_sem,
    back_sem,
    home_sem,
):
    outs = (out0, out1, out2, out3, out4, out5)
    ins = (in0, in1, in2, in3, in4, in5)
    backs = (back0, back1, back2, back3, back4, back5)
    homes = (home0, home1, home2, home3, home4, home5)
    mixes = (w0, mix1, mix2, mix3, mix4)

    at_x = lax.axis_index("gx")
    at_y = lax.axis_index("gy")

    def cell(index, sign):
        step_x, step_y = DIRECTIONS[index]
        return (
            lax.rem(at_x + (sign * step_x + count_x), count_x),
            lax.rem(at_y + (sign * step_y + count_y), count_y),
        )

    def pieces(order):
        return (0, 5) if order == 0 else (order,)

    def stage(buffers, order, value):
        lanes = SPANS[order][2]
        value = value.reshape(8, GHOST, SPANS[order][1])
        buffers[order][...] = value[:, :, 0:lanes].astype(BF16)
        if order == 0:
            left = value[:, :, lanes:]
            half = GHOST // 2
            buffers[5][...] = jnp.concatenate(
                [left[:, 0:half], left[:, half:]], axis=2
            ).astype(BF16)

    def staged(buffers, order):
        lanes = SPANS[order][2]
        value = buffers[order][...].reshape(GHOSTS, lanes)
        if order == 0:
            packed = buffers[5][...].astype(F32)
            left = jnp.concatenate([packed[:, :, 0:CH], packed[:, :, CH:]], axis=1)
            left = left.reshape(GHOSTS, CH).astype(BF16)
            value = jnp.concatenate([value, left], axis=1)
        return value

    feat_loads = {
        order: pltpu.make_async_copy(
            feat_hbm.at[SPANS[order][0] : SPANS[order][0] + SPANS[order][1]],
            feat.at[SPANS[order][0] : SPANS[order][0] + SPANS[order][1]],
            feat_sem.at[order],
        )
        for order in ORDER
    }
    loads = [
        pltpu.make_async_copy(source, target, local_sem.at[number])
        for number, (source, target) in enumerate(
            (
                (list_hbm, list_ref),
                (source_hbm, source_ref),
                (target_hbm, target_ref),
                (harm_hbm.at[:, 0], harm),
                (tg_hbm, tg),
                (fg_hbm, fg),
                (cot_hbm, cot),
                (w0_hbm, w0),
                (w1_hbm, w1),
                (w2_hbm, w2),
                (w3_hbm, w3),
                (w4_hbm, w4),
            )
        )
    ]
    for load in (loads[0], *feat_loads.values(), *loads[1:]):
        load.start()

    barrier = pltpu.get_barrier_semaphore()
    for index in range(8):
        pl.semaphore_signal(barrier, inc=1, device_id=cell(index, 1), device_id_type=MESH)

    loads[0].wait()
    list_row = nn(
        list_ref[...].astype(F32).astype(BF16),
        ones_where(iota((GHOST, GHOSTS), 0) == (iota((GHOST, GHOSTS), 1) & 31)).astype(BF16),
    )
    list_row = jnp.where(iota((8, GHOSTS), 0) == (iota((8, GHOSTS), 1) >> 5), list_row, 0.0)
    list_row = jnp.sum(list_row, axis=0, keepdims=True)
    pick_list[...] = ones_where(iota((ATOMS, GHOSTS), 0).astype(F32) == list_row).astype(BF16)
    eye = identity(256)
    pick_list_t = nt(eye, pick_list[...]).astype(BF16)

    lending = {}
    returning = {}
    waiting = None
    started = False

    def lend(order, directions):
        for index in directions:
            for piece in pieces(order):
                copy = pltpu.make_async_remote_copy(
                    src_ref=outs[piece].at[index],
                    dst_ref=ins[piece].at[index],
                    send_sem=out_sem.at[piece, index],
                    recv_sem=in_sem.at[piece, index],
                    device_id=cell(index, -1),
                    device_id_type=MESH,
                )
                copy.start()
                lending[piece, index] = copy

    def give_back(order, directions):
        for index in directions:
            for piece in pieces(order):
                copy = pltpu.make_async_remote_copy(
                    src_ref=backs[piece].at[index],
                    dst_ref=homes[piece].at[index],
                    send_sem=back_sem.at[piece, index],
                    recv_sem=home_sem.at[piece, index],
                    device_id=cell(index, 1),
                    device_id_type=MESH,
                )
                copy.start()
                returning[piece, index] = copy

    for order in ORDER:
        first, rows, lanes = SPANS[order]
        feat_loads[order].wait()
        stage(outs, order, nt(pick_list_t, feat[first : first + rows, :]))
        if not started:
            pl.semaphore_wait(barrier, 8)
            started = True
        lend(order, LEND_FIRST)

    for order in ORDER:
        lend(order, LEND_REST)

    loads[1].wait()
    loads[2].wait()
    pick_source[...] = ones_where(
        iota((ATOMS + GHOSTS, EDGES), 0) == source_ref[...]
    ).astype(BF16)
    pick_target[...] = ones_where(iota((ATOMS, EDGES), 0) == target_ref[...]).astype(BF16)
    pick_source_t[...] = nt(eye, pick_source[...]).astype(BF16)
    pick_target_t[...] = nt(eye, pick_target[...]).astype(BF16)

    loads[3].wait()
    harm_parts = [nt(eye, piece).astype(BF16) for piece in parts(harm[...], 3)]
    for order in ORDER:
        first, rows, lanes = SPANS[order]
        spread = ones_where(
            ((iota((COEFS, rows), 1) + first) >> 6) == iota((COEFS, rows), 0)
        ).astype(BF16)
        wide = nn(harm_parts[0], spread) + nn(harm_parts[1], spread) + nn(harm_parts[2], spread)
        harm_t[:, first : first + rows] = wide

    loads[4].wait()
    loads[5].wait()
    grid_rows = ones_where((iota((GRID * 8, GRID), 0) >> 3) == iota((GRID * 8, GRID), 1)).astype(BF16)
    grid_cols = ones_where((iota((GRID, GRID * 8), 1) >> 3) == iota((GRID, GRID * 8), 0)).astype(BF16)
    coef_rows = ones_where((iota((COEFS * 8, COEFS), 0) >> 3) == iota((COEFS * 8, COEFS), 1)).astype(BF16)
    coef_cols = ones_where((iota((COEFS, COEFS * 8), 1) >> 3) == iota((COEFS, COEFS * 8), 0)).astype(BF16)
    tall = (iota((GRID * 8, COEFS * 8), 0) & 7) == (iota((GRID * 8, COEFS * 8), 1) & 7)
    flat = (iota((COEFS * 8, GRID * 8), 0) & 7) == (iota((COEFS * 8, GRID * 8), 1) & 7)
    for number, (to_part, from_part) in enumerate(zip(parts(tg[...], 2), parts(fg[...], 2))):
        kron_a[number] = jnp.where(
            tall, nn(nt(grid_rows, to_part).astype(BF16), coef_cols), 0.0
        ).astype(BF16)
        kron_at[number] = jnp.where(
            flat, nn(nn(coef_rows, to_part).astype(BF16), grid_cols), 0.0
        ).astype(BF16)
        kron_b[number] = jnp.where(
            flat, nn(nn(coef_rows, from_part).astype(BF16), grid_cols), 0.0
        ).astype(BF16)
        kron_bt[number] = jnp.where(
            tall, nn(nt(grid_rows, from_part).astype(BF16), coef_cols), 0.0
        ).astype(BF16)

    feat32[...] = feat[...].astype(F32).reshape(COEFS, 8, 8, ATOMS)
    loads[6].wait()
    cot32[...] = cot[...].astype(F32).reshape(COEFS, 8, 8, ATOMS)

    def pair(ref, at):
        return jnp.concatenate(
            [ref[:, 2 * at + side].reshape(COEFS * 8, ATOMS) for side in range(2)], axis=1
        )

    def unpair(ref, at, value):
        for side in range(2):
            ref[:, 2 * at + side] = value[:, side * ATOMS : (side + 1) * ATOMS].reshape(
                COEFS, 8, ATOMS
            )

    def times(kron, value, stripe):
        high, low = parts(value, 2)
        return (
            nn(kron[0, :, stripe], high) + nn(kron[1, :, stripe], high) + nn(kron[0, :, stripe], low)
        )

    @pl.loop(0, 4)
    def _(at):
        feat_pair = pair(feat32, at).astype(BF16)
        grid_feat[at] = nn(kron_a[0], feat_pair) + nn(kron_a[1], feat_pair)
        cot_pair = pair(cot32, at).astype(BF16)
        d_product[at] = nn(kron_bt[0], cot_pair) + nn(kron_bt[1], cot_pair)
        joint[at] = (0.5 * EDGE_NORM) * grid_feat[at] * d_product[at]

    for number in range(7, 12):
        loads[number].wait()
    for weight, mix in ((w1, mix1), (w2, mix2), (w3, mix3), (w4, mix4)):
        size = weight.shape[1]
        left = ones_where(iota((size, 2 * size), 0) == iota((size, 2 * size), 1)).astype(BF16)
        right = ones_where(iota((size, 2 * size), 0) + size == iota((size, 2 * size), 1)).astype(BF16)
        mix[0:size, :] = (nn(weight[0], left) - nn(weight[1], right)).astype(BF16)
        mix[size : 2 * size, :] = (nn(weight[1], left) + nn(weight[0], right)).astype(BF16)

    for order in ORDER:
        first, rows, lanes = SPANS[order]
        columns = nt(pick_source_t[:, 0:ATOMS], feat[first : first + rows, :])
        for index in SEND_DIRS:
            for piece in pieces(order):
                lending[piece, index].wait_recv()
        columns = columns + nn(pick_source_t[:, ATOMS:], staged(ins, order))
        filtered = (columns * harm_t[:, first : first + rows]).astype(BF16)
        message = nt(mixes[order][...], filtered)
        high, low = parts(message, 2)
        total = nt(high, pick_target[...]) + nt(low, pick_target[...])
        agg[first // CH : (first + rows) // CH] = (total * (0.5 * EDGE_NORM)).reshape(
            rows // CH, 8, 8, ATOMS
        )

    @pl.loop(0, 4)
    def _(at):
        agg_pair = pair(agg, at).astype(BF16)
        total = None
        for begin, size in STRIPES:
            stripe = slice(begin, begin + size)
            rough = nn(kron_a[0, stripe, :], agg_pair)
            grid_agg[at, stripe, :] = rough
            turn = jnp.tanh(rough)
            slope = (1.0 + turn) * (1.0 + rough * (1.0 - turn))
            term = nn(kron_at[0, :, stripe], (joint[at, stripe, :] * slope).astype(BF16))
            total = term if total is None else total + term
        unpair(d_agg, at, total)

    for order in BACK_ORDER:
        first, rows, lanes = SPANS[order]
        d_rows = d_agg[first // CH : (first + rows) // CH].reshape(rows, ATOMS).astype(BF16)
        d_message = nt(pick_target_t[...], d_rows).astype(BF16)
        d_filtered = nn(d_message, mixes[order][...])
        high, low = parts(d_filtered * harm_t[:, first : first + rows], 2)
        ghosts = nn(pick_source[ATOMS:, :], high)
        stage(backs, order, ghosts)
        give_back(order, RETURN_FIRST)
        if waiting is not None:
            give_back(waiting, RETURN_REST)
        waiting = order
        if order == BACK_ORDER[0]:
            give_back(waiting, RETURN_REST)
            waiting = None
        own_t[:, first : first + rows] = nn(pick_source[0:ATOMS, :], high) + nn(
            pick_source[0:ATOMS, :], low
        )

    give_back(waiting, RETURN_REST)

    @pl.loop(0, 4)
    def _(at):
        agg_high, agg_low = parts(pair(agg, at), 2)
        update = None
        for begin, size in STRIPES:
            stripe = slice(begin, begin + size)
            exact = (
                grid_agg[at, stripe, :]
                + nn(kron_a[1, stripe, :], agg_high)
                + nn(kron_a[0, stripe, :], agg_low)
            )
            exact = exact + exact
            active = exact * jax.nn.sigmoid(exact)
            made = times(kron_b, active * grid_feat[at, stripe, :], stripe)
            back = times(kron_at, active * d_product[at, stripe, :], stripe)
            update = made if update is None else update + made
            d_node = back if begin == 0 else d_node + back
        unpair(feat32, at, pair(feat32, at) + update)
        unpair(cot32, at, pair(cot32, at) + d_node)

    layer_ref[...] = feat32[...].reshape(ROWS, ATOMS).astype(BF16)

    for order in BACK_ORDER:
        first, rows, lanes = SPANS[order]
        for index in SEND_DIRS:
            for piece in pieces(order):
                returning[piece, index].wait_recv()
        arrived = staged(homes, order)
        total = own_t[:, first : first + rows] + nn(pick_list[...], arrived)
        node = cot32[first // CH : (first + rows) // CH].reshape(rows, ATOMS)
        grad_ref[first : first + rows, :] = node + jnp.transpose(total)

    for copy in (*lending.values(), *returning.values()):
        copy.wait_send()


def store_kernel(layer_ref, grad_ref, layer_hbm, grad_hbm, sem):
    copies = [
        pltpu.make_async_copy(layer_ref, layer_hbm, sem.at[0]),
        pltpu.make_async_copy(grad_ref, grad_hbm, sem.at[1]),
    ]
    for copy in copies:
        copy.start()
    for copy in copies:
        copy.wait()


def per_device(
    features,
    cotangent,
    w_order0,
    w_order1,
    w_order2,
    w_order3,
    w_order4,
    to_grid,
    from_grid,
    edge_harmonics,
    edge_source,
    edge_target,
    send_list,
):
    count_x = lax.axis_size("gx")
    count_y = lax.axis_size("gy")
    in_hbm = pl.BlockSpec(memory_space=pltpu.HBM)
    vmem = pl.BlockSpec(memory_space=pltpu.VMEM)
    grids = pltpu.VMEM((4, GRID * 8, 2 * ATOMS), F32)
    tiles = pltpu.VMEM((COEFS, 8, 8, ATOMS), F32)
    tall = pltpu.VMEM((2, GRID * 8, COEFS * 8), BF16)
    flat = pltpu.VMEM((2, COEFS * 8, GRID * 8), BF16)
    blocks = [pltpu.VMEM((8, GHOST, lanes), BF16) for _, _, lanes in SPANS]
    blocks.append(pltpu.VMEM((8, GHOST // 2, ATOMS), BF16))
    copies = pltpu.SemaphoreType.DMA((6, 8))
    layer, grad = pl.pallas_call(
        functools.partial(kernel, count_x, count_y),
        out_shape=(
            jax.ShapeDtypeStruct((ROWS, ATOMS), BF16),
            jax.ShapeDtypeStruct((ROWS, ATOMS), F32),
        ),
        in_specs=[in_hbm] * 13,
        out_specs=(vmem, vmem),
        scratch_shapes=[
            pltpu.VMEM((ROWS, ATOMS), BF16),
            pltpu.VMEM((ROWS, ATOMS), BF16),
            pltpu.VMEM(w_order0.shape, BF16),
            pltpu.VMEM(w_order1.shape, BF16),
            pltpu.VMEM(w_order2.shape, BF16),
            pltpu.VMEM(w_order3.shape, BF16),
            pltpu.VMEM(w_order4.shape, BF16),
            pltpu.VMEM((COEFS, GRID), F32),
            pltpu.VMEM((COEFS, GRID), F32),
            pltpu.VMEM((COEFS, EDGES), F32),
            pltpu.VMEM((1, EDGES), jnp.int32),
            pltpu.VMEM((1, EDGES), jnp.int32),
            pltpu.VMEM((8, GHOST), jnp.int32),
            tiles,
            tiles,
            *blocks,
            *blocks,
            *blocks,
            *blocks,
            *[pltpu.VMEM((rows, rows), BF16) for _, rows, _ in SPANS[1:]],
            pltpu.VMEM((EDGES, ROWS), F32),
            pltpu.VMEM((ATOMS, GHOSTS), BF16),
            pltpu.VMEM((ATOMS + GHOSTS, EDGES), BF16),
            pltpu.VMEM((EDGES, ATOMS + GHOSTS), BF16),
            pltpu.VMEM((ATOMS, EDGES), BF16),
            pltpu.VMEM((EDGES, ATOMS), BF16),
            tall,
            flat,
            flat,
            tall,
            grids,
            grids,
            grids,
            grids,
            tiles,
            tiles,
            pltpu.VMEM((ATOMS, ROWS), F32),
            pltpu.SemaphoreType.DMA((12,)),
            pltpu.SemaphoreType.DMA((5,)),
            copies,
            copies,
            copies,
            copies,
        ],
        compiler_params=pltpu.CompilerParams(
            collective_id=0, has_side_effects=True, vmem_limit_bytes=40 * 1024 * 1024
        ),
        name="layer",
    )(
        *[
            pltpu.with_memory_space_constraint(value, pltpu.HBM)
            for value in (
                features[0, 0],
                cotangent[0, 0],
                w_order0,
                w_order1,
                w_order2,
                w_order3,
                w_order4,
                to_grid.T,
                from_grid,
                edge_harmonics[0, 0].reshape(COEFS, 1, EDGES),
                edge_source[0],
                edge_target[0],
                send_list[0, 0],
            )
        ],
    )
    layer, grad = pl.pallas_call(
        store_kernel,
        out_shape=(
            jax.ShapeDtypeStruct((ROWS, ATOMS), BF16),
            jax.ShapeDtypeStruct((ROWS, ATOMS), F32),
        ),
        in_specs=[vmem, vmem],
        out_specs=(in_hbm, in_hbm),
        scratch_shapes=[pltpu.SemaphoreType.DMA((2,))],
        compiler_params=pltpu.CompilerParams(vmem_limit_bytes=4 * 1024 * 1024),
        name="store",
    )(layer, grad)
    return layer[None, None], grad[None, None]


def solution(mesh):
    cells = P("gx", "gy", None, None)
    placed = (cells, cells, P(), P(), P(), P(), P(), P(), P(), cells, P("gx", "gy", None), P("gx", "gy", None), cells)
    return jax.shard_map(
        per_device,
        mesh=mesh,
        in_specs=placed,
        out_specs=(cells, cells),
        check_vma=False,
    )
```

```python
import functools

import jax
import jax.numpy as jnp
from jax import lax
from jax.experimental import pallas as pl
from jax.experimental.pallas import tpu as pltpu
from jax.sharding import PartitionSpec as P

DIRECTIONS = ((-1, -1), (-1, 0), (-1, 1), (0, -1), (0, 1), (1, -1), (1, 0), (1, 1))
EDGE_NORM = 0.35
MESH = pl.DeviceIdType.MESH
F32 = jnp.float32
BF16 = jnp.bfloat16

COEFS = 25
CH = 64
GRID = 100
ATOMS = 128
EDGES = 256
GHOST = 32
ROWS = COEFS * CH
GHOSTS = 8 * GHOST
SPANS = ((0, 320), (320, 512), (832, 384), (1216, 256), (1472, 128))
PLACES = ((0, 80), (80, 128), (272, 96), (208, 64), (368, 32))
WIRE = 400
LEND_PIECES = ((0, 1, 3), (2,), (4,))
BACK_PIECES = ((4,), (0,), (1,), (2,), (3,))
STRIPES = ((0, 256), (256, 256), (512, 256), (768, 32))
SEND_DIRS = (0, 2, 5, 7, 1, 6, 3, 4)


def nn(left, right):
    return jnp.dot(left, right, preferred_element_type=F32)


def nt(left, right):
    return lax.dot_general(left, right, (((1,), (1,)), ((), ())), preferred_element_type=F32)


def parts(value, count):
    pieces = []
    for _ in range(count - 1):
        piece = value.astype(BF16)
        pieces.append(piece)
        value = value - piece.astype(F32)
    pieces.append(value.astype(BF16))
    return pieces


def iota(shape, dim):
    return lax.broadcasted_iota(jnp.int32, shape, dim)


def ones_where(mask):
    return jnp.where(mask, 1.0, 0.0).astype(F32)


def identity(size):
    return ones_where(iota((size, size), 0) == iota((size, size), 1)).astype(BF16)


def kernel(
    count_x,
    count_y,
    feat_hbm,
    cot_hbm,
    w0_hbm,
    w1_hbm,
    w2_hbm,
    w3_hbm,
    w4_hbm,
    tg_hbm,
    fg_hbm,
    harm_hbm,
    source_hbm,
    target_hbm,
    list_hbm,
    layer_ref,
    grad_ref,
    feat,
    cot,
    w0,
    w1,
    w2,
    w3,
    w4,
    tg,
    fg,
    harm,
    source_ref,
    target_ref,
    list_ref,
    feat32,
    cot32,
    outs,
    ins,
    backs,
    homes,
    mix1,
    mix2,
    mix3,
    mix4,
    harm_t,
    pick_list,
    pick_source,
    pick_source_t,
    pick_target,
    pick_target_t,
    kron_a,
    kron_at,
    kron_b,
    kron_bt,
    grid_feat,
    d_product,
    grid_agg,
    joint,
    agg,
    d_agg,
    own_t,
    local_sem,
    feat_sem,
    out_sem,
    in_sem,
    back_sem,
    home_sem,
):
    mixes = (w0, mix1, mix2, mix3, mix4)

    at_x = lax.axis_index("gx")
    at_y = lax.axis_index("gy")

    def cell(index, sign):
        step_x, step_y = DIRECTIONS[index]
        return (
            lax.rem(at_x + (sign * step_x + count_x), count_x),
            lax.rem(at_y + (sign * step_y + count_y), count_y),
        )

    def stage(buffer, order, value):
        begin, _ = PLACES[order]
        rows = SPANS[order][1]
        value = value.reshape(8, GHOST, rows)
        for at in range(0, rows - ATOMS + 1, ATOMS):
            buffer[:, begin : begin + GHOST, :] = value[:, :, at : at + ATOMS].astype(BF16)
            begin += GHOST
        if rows % ATOMS:
            left = value[:, :, rows - CH :]
            half = GHOST // 2
            buffer[:, begin : begin + half, :] = jnp.concatenate(
                [left[:, 0:half], left[:, half:]], axis=2
            ).astype(BF16)

    def staged(buffer, order):
        begin, _ = PLACES[order]
        rows = SPANS[order][1]
        tiles = []
        for _ in range(rows // ATOMS):
            tiles.append(buffer[:, begin : begin + GHOST, :].reshape(GHOSTS, ATOMS))
            begin += GHOST
        if rows % ATOMS:
            packed = buffer[:, begin : begin + GHOST // 2, :].astype(F32)
            left = jnp.concatenate([packed[:, :, 0:CH], packed[:, :, CH:]], axis=1)
            tiles.append(left.reshape(GHOSTS, CH).astype(BF16))
        return jnp.concatenate(tiles, axis=1) if len(tiles) > 1 else tiles[0]

    def exchange(piece, number, source, target, send_sem, recv_sem, sign):
        begin = PLACES[piece[0]][0]
        end = sum(PLACES[piece[-1]])
        copies = [
            pltpu.make_async_remote_copy(
                src_ref=source.at[index, begin:end],
                dst_ref=target.at[index, begin:end],
                send_sem=send_sem.at[number, index],
                recv_sem=recv_sem.at[number, index],
                device_id=cell(index, sign),
                device_id_type=MESH,
            )
            for index in SEND_DIRS
        ]
        for copy in copies:
            copy.start()
        return copies

    feat_loads = {
        order: pltpu.make_async_copy(
            feat_hbm.at[SPANS[order][0] : SPANS[order][0] + SPANS[order][1]],
            feat.at[SPANS[order][0] : SPANS[order][0] + SPANS[order][1]],
            feat_sem.at[order],
        )
        for order in range(5)
    }
    loads = [
        pltpu.make_async_copy(source, target, local_sem.at[number])
        for number, (source, target) in enumerate(
            (
                (list_hbm, list_ref),
                (source_hbm, source_ref),
                (target_hbm, target_ref),
                (harm_hbm.at[:, 0], harm),
                (tg_hbm, tg),
                (fg_hbm, fg),
                (cot_hbm, cot),
                (w0_hbm, w0),
                (w1_hbm, w1),
                (w2_hbm, w2),
                (w3_hbm, w3),
                (w4_hbm, w4),
            )
        )
    ]
    for load in (loads[0], *feat_loads.values(), *loads[1:]):
        load.start()

    barrier = pltpu.get_barrier_semaphore()
    for index in range(8):
        pl.semaphore_signal(barrier, inc=1, device_id=cell(index, 1), device_id_type=MESH)

    loads[0].wait()
    list_row = nn(
        list_ref[...].astype(F32).astype(BF16),
        ones_where(iota((GHOST, GHOSTS), 0) == (iota((GHOST, GHOSTS), 1) & 31)).astype(BF16),
    )
    list_row = jnp.where(iota((8, GHOSTS), 0) == (iota((8, GHOSTS), 1) >> 5), list_row, 0.0)
    list_row = jnp.sum(list_row, axis=0, keepdims=True)
    pick_list[...] = ones_where(iota((ATOMS, GHOSTS), 0).astype(F32) == list_row).astype(BF16)
    eye = identity(256)
    pick_list_t = nt(eye, pick_list[...]).astype(BF16)

    lending = []
    for number, piece in enumerate(LEND_PIECES):
        for order in piece:
            first, rows = SPANS[order]
            feat_loads[order].wait()
            stage(outs, order, nt(pick_list_t, feat[first : first + rows, :]))
        if number == 0:
            pl.semaphore_wait(barrier, 8)
        lending.append(exchange(piece, number, outs, ins, out_sem, in_sem, -1))

    loads[1].wait()
    loads[2].wait()
    pick_source[...] = ones_where(
        iota((ATOMS + GHOSTS, EDGES), 0) == source_ref[...]
    ).astype(BF16)
    pick_target[...] = ones_where(iota((ATOMS, EDGES), 0) == target_ref[...]).astype(BF16)
    pick_source_t[...] = nt(eye, pick_source[...]).astype(BF16)
    pick_target_t[...] = nt(eye, pick_target[...]).astype(BF16)

    loads[3].wait()
    harm_parts = [nt(eye, piece).astype(BF16) for piece in parts(harm[...], 3)]
    for order in range(5):
        first, rows = SPANS[order]
        spread = ones_where(
            ((iota((COEFS, rows), 1) + first) >> 6) == iota((COEFS, rows), 0)
        ).astype(BF16)
        wide = nn(harm_parts[0], spread) + nn(harm_parts[1], spread) + nn(harm_parts[2], spread)
        harm_t[:, first : first + rows] = wide

    loads[4].wait()
    loads[5].wait()
    grid_rows = ones_where((iota((GRID * 8, GRID), 0) >> 3) == iota((GRID * 8, GRID), 1)).astype(BF16)
    grid_cols = ones_where((iota((GRID, GRID * 8), 1) >> 3) == iota((GRID, GRID * 8), 0)).astype(BF16)
    coef_rows = ones_where((iota((COEFS * 8, COEFS), 0) >> 3) == iota((COEFS * 8, COEFS), 1)).astype(BF16)
    coef_cols = ones_where((iota((COEFS, COEFS * 8), 1) >> 3) == iota((COEFS, COEFS * 8), 0)).astype(BF16)
    tall = (iota((GRID * 8, COEFS * 8), 0) & 7) == (iota((GRID * 8, COEFS * 8), 1) & 7)
    flat = (iota((COEFS * 8, GRID * 8), 0) & 7) == (iota((COEFS * 8, GRID * 8), 1) & 7)
    for number, (to_part, from_part) in enumerate(zip(parts(tg[...], 2), parts(fg[...], 2))):
        kron_a[number] = jnp.where(
            tall, nn(nt(grid_rows, to_part).astype(BF16), coef_cols), 0.0
        ).astype(BF16)
        kron_at[number] = jnp.where(
            flat, nn(nn(coef_rows, to_part).astype(BF16), grid_cols), 0.0
        ).astype(BF16)
        kron_b[number] = jnp.where(
            flat, nn(nn(coef_rows, from_part).astype(BF16), grid_cols), 0.0
        ).astype(BF16)
        kron_bt[number] = jnp.where(
            tall, nn(nt(grid_rows, from_part).astype(BF16), coef_cols), 0.0
        ).astype(BF16)

    feat32[...] = feat[...].astype(F32).reshape(COEFS, 8, 8, ATOMS)
    loads[6].wait()
    cot32[...] = cot[...].astype(F32).reshape(COEFS, 8, 8, ATOMS)

    def pair(ref, at):
        return jnp.concatenate(
            [ref[:, 2 * at + side].reshape(COEFS * 8, ATOMS) for side in range(2)], axis=1
        )

    def unpair(ref, at, value):
        for side in range(2):
            ref[:, 2 * at + side] = value[:, side * ATOMS : (side + 1) * ATOMS].reshape(
                COEFS, 8, ATOMS
            )

    def times(kron, value, stripe):
        high, low = parts(value, 2)
        return (
            nn(kron[0, :, stripe], high) + nn(kron[1, :, stripe], high) + nn(kron[0, :, stripe], low)
        )

    @pl.loop(0, 4)
    def _(at):
        feat_pair = pair(feat32, at).astype(BF16)
        grid_feat[at] = nn(kron_a[0], feat_pair) + nn(kron_a[1], feat_pair)
        cot_pair = pair(cot32, at).astype(BF16)
        d_product[at] = nn(kron_bt[0], cot_pair) + nn(kron_bt[1], cot_pair)
        joint[at] = (0.5 * EDGE_NORM) * grid_feat[at] * d_product[at]

    for number in range(7, 12):
        loads[number].wait()
    for weight, mix in ((w1, mix1), (w2, mix2), (w3, mix3), (w4, mix4)):
        size = weight.shape[1]
        left = ones_where(iota((size, 2 * size), 0) == iota((size, 2 * size), 1)).astype(BF16)
        right = ones_where(iota((size, 2 * size), 0) + size == iota((size, 2 * size), 1)).astype(BF16)
        mix[0:size, :] = (nn(weight[0], left) - nn(weight[1], right)).astype(BF16)
        mix[size : 2 * size, :] = (nn(weight[1], left) + nn(weight[0], right)).astype(BF16)

    for piece, copies in zip(LEND_PIECES, lending):
        ready = False
        for order in piece:
            first, rows = SPANS[order]
            columns = nt(pick_source_t[:, 0:ATOMS], feat[first : first + rows, :])
            if not ready:
                for copy in copies:
                    copy.wait_recv()
                ready = True
            columns = columns + nn(pick_source_t[:, ATOMS:], staged(ins, order))
            filtered = (columns * harm_t[:, first : first + rows]).astype(BF16)
            message = nt(mixes[order][...], filtered)
            high, low = parts(message, 2)
            total = nt(high, pick_target[...]) + nt(low, pick_target[...])
            agg[first // CH : (first + rows) // CH] = (total * (0.5 * EDGE_NORM)).reshape(
                rows // CH, 8, 8, ATOMS
            )

    @pl.loop(0, 4)
    def _(at):
        agg_pair = pair(agg, at).astype(BF16)
        total = None
        for begin, size in STRIPES:
            stripe = slice(begin, begin + size)
            rough = nn(kron_a[0, stripe, :], agg_pair)
            grid_agg[at, stripe, :] = rough
            turn = jnp.tanh(rough)
            slope = (1.0 + turn) * (1.0 + rough * (1.0 - turn))
            term = nn(kron_at[0, :, stripe], (joint[at, stripe, :] * slope).astype(BF16))
            total = term if total is None else total + term
        unpair(d_agg, at, total)

    returning = []
    for number, piece in enumerate(BACK_PIECES):
        order = piece[0]
        first, rows = SPANS[order]
        d_rows = d_agg[first // CH : (first + rows) // CH].reshape(rows, ATOMS).astype(BF16)
        d_message = nt(pick_target_t[...], d_rows).astype(BF16)
        d_filtered = nn(d_message, mixes[order][...])
        high, low = parts(d_filtered * harm_t[:, first : first + rows], 2)
        ghosts = nn(pick_source[ATOMS:, :], high)
        stage(backs, order, ghosts)
        returning.append(exchange(piece, number, backs, homes, back_sem, home_sem, 1))
        own_t[:, first : first + rows] = nn(pick_source[0:ATOMS, :], high) + nn(
            pick_source[0:ATOMS, :], low
        )

    @pl.loop(0, 4)
    def _(at):
        agg_high, agg_low = parts(pair(agg, at), 2)
        update = None
        for begin, size in STRIPES:
            stripe = slice(begin, begin + size)
            exact = (
                grid_agg[at, stripe, :]
                + nn(kron_a[1, stripe, :], agg_high)
                + nn(kron_a[0, stripe, :], agg_low)
            )
            exact = exact + exact
            active = exact * jax.nn.sigmoid(exact)
            made = times(kron_b, active * grid_feat[at, stripe, :], stripe)
            back = times(kron_at, active * d_product[at, stripe, :], stripe)
            update = made if update is None else update + made
            d_node = back if begin == 0 else d_node + back
        unpair(feat32, at, pair(feat32, at) + update)
        unpair(cot32, at, pair(cot32, at) + d_node)

    layer_ref[...] = feat32[...].reshape(ROWS, ATOMS).astype(BF16)

    for (order,), copies in zip(BACK_PIECES, returning):
        first, rows = SPANS[order]
        for copy in copies:
            copy.wait_recv()
        arrived = staged(homes, order)
        total = own_t[:, first : first + rows] + nn(pick_list[...], arrived)
        node = cot32[first // CH : (first + rows) // CH].reshape(rows, ATOMS)
        grad_ref[first : first + rows, :] = node + jnp.transpose(total)

    for copies in (*lending, *returning):
        for copy in copies:
            copy.wait_send()


def store_kernel(layer_ref, grad_ref, layer_hbm, grad_hbm, sem):
    copies = [
        pltpu.make_async_copy(layer_ref, layer_hbm, sem.at[0]),
        pltpu.make_async_copy(grad_ref, grad_hbm, sem.at[1]),
    ]
    for copy in copies:
        copy.start()
    for copy in copies:
        copy.wait()


def per_device(
    features,
    cotangent,
    w_order0,
    w_order1,
    w_order2,
    w_order3,
    w_order4,
    to_grid,
    from_grid,
    edge_harmonics,
    edge_source,
    edge_target,
    send_list,
):
    count_x = lax.axis_size("gx")
    count_y = lax.axis_size("gy")
    in_hbm = pl.BlockSpec(memory_space=pltpu.HBM)
    vmem = pl.BlockSpec(memory_space=pltpu.VMEM)
    grids = pltpu.VMEM((4, GRID * 8, 2 * ATOMS), F32)
    tiles = pltpu.VMEM((COEFS, 8, 8, ATOMS), F32)
    tall = pltpu.VMEM((2, GRID * 8, COEFS * 8), BF16)
    flat = pltpu.VMEM((2, COEFS * 8, GRID * 8), BF16)
    blocks = pltpu.VMEM((8, WIRE, ATOMS), BF16)
    lend_sems = pltpu.SemaphoreType.DMA((len(LEND_PIECES), 8))
    back_sems = pltpu.SemaphoreType.DMA((len(BACK_PIECES), 8))
    layer, grad = pl.pallas_call(
        functools.partial(kernel, count_x, count_y),
        out_shape=(
            jax.ShapeDtypeStruct((ROWS, ATOMS), BF16),
            jax.ShapeDtypeStruct((ROWS, ATOMS), F32),
        ),
        in_specs=[in_hbm] * 13,
        out_specs=(vmem, vmem),
        scratch_shapes=[
            pltpu.VMEM((ROWS, ATOMS), BF16),
            pltpu.VMEM((ROWS, ATOMS), BF16),
            pltpu.VMEM(w_order0.shape, BF16),
            pltpu.VMEM(w_order1.shape, BF16),
            pltpu.VMEM(w_order2.shape, BF16),
            pltpu.VMEM(w_order3.shape, BF16),
            pltpu.VMEM(w_order4.shape, BF16),
            pltpu.VMEM((COEFS, GRID), F32),
            pltpu.VMEM((COEFS, GRID), F32),
            pltpu.VMEM((COEFS, EDGES), F32),
            pltpu.VMEM((1, EDGES), jnp.int32),
            pltpu.VMEM((1, EDGES), jnp.int32),
            pltpu.VMEM((8, GHOST), jnp.int32),
            tiles,
            tiles,
            blocks,
            blocks,
            blocks,
            blocks,
            *[pltpu.VMEM((rows, rows), BF16) for _, rows in SPANS[1:]],
            pltpu.VMEM((EDGES, ROWS), F32),
            pltpu.VMEM((ATOMS, GHOSTS), BF16),
            pltpu.VMEM((ATOMS + GHOSTS, EDGES), BF16),
            pltpu.VMEM((EDGES, ATOMS + GHOSTS), BF16),
            pltpu.VMEM((ATOMS, EDGES), BF16),
            pltpu.VMEM((EDGES, ATOMS), BF16),
            tall,
            flat,
            flat,
            tall,
            grids,
            grids,
            grids,
            grids,
            tiles,
            tiles,
            pltpu.VMEM((ATOMS, ROWS), F32),
            pltpu.SemaphoreType.DMA((12,)),
            pltpu.SemaphoreType.DMA((5,)),
            lend_sems,
            lend_sems,
            back_sems,
            back_sems,
        ],
        compiler_params=pltpu.CompilerParams(
            collective_id=0, has_side_effects=True, vmem_limit_bytes=40 * 1024 * 1024
        ),
        name="layer",
    )(
        *[
            pltpu.with_memory_space_constraint(value, pltpu.HBM)
            for value in (
                features[0, 0],
                cotangent[0, 0],
                w_order0,
                w_order1,
                w_order2,
                w_order3,
                w_order4,
                to_grid.T,
                from_grid,
                edge_harmonics[0, 0].reshape(COEFS, 1, EDGES),
                edge_source[0],
                edge_target[0],
                send_list[0, 0],
            )
        ],
    )
    layer, grad = pl.pallas_call(
        store_kernel,
        out_shape=(
            jax.ShapeDtypeStruct((ROWS, ATOMS), BF16),
            jax.ShapeDtypeStruct((ROWS, ATOMS), F32),
        ),
        in_specs=[vmem, vmem],
        out_specs=(in_hbm, in_hbm),
        scratch_shapes=[pltpu.SemaphoreType.DMA((2,))],
        compiler_params=pltpu.CompilerParams(vmem_limit_bytes=4 * 1024 * 1024),
        name="store",
    )(layer, grad)
    return layer[None, None], grad[None, None]


def solution(mesh):
    cells = P("gx", "gy", None, None)
    placed = (cells, cells, P(), P(), P(), P(), P(), P(), P(), cells, P("gx", "gy", None), P("gx", "gy", None), cells)
    return jax.shard_map(
        per_device,
        mesh=mesh,
        in_specs=placed,
        out_specs=(cells, cells),
        check_vma=False,
    )
```

```python
import functools

import jax
import jax.numpy as jnp
from jax import lax
from jax.experimental import pallas as pl
from jax.experimental.pallas import tpu as pltpu
from jax.sharding import PartitionSpec as P

DIRECTIONS = ((-1, -1), (-1, 0), (-1, 1), (0, -1), (0, 1), (1, -1), (1, 0), (1, 1))
EDGE_NORM = 0.35
MESH = pl.DeviceIdType.MESH
F32 = jnp.float32
BF16 = jnp.bfloat16

COEFS = 25
CH = 64
GRID = 100
ATOMS = 128
EDGES = 256
GHOST = 32
ROWS = COEFS * CH
GHOSTS = 8 * GHOST
SPANS = ((0, 320), (320, 512), (832, 384), (1216, 256), (1472, 128))
PLACES = ((0, 80), (80, 128), (272, 96), (208, 64), (368, 32))
WIRE = 400
LEND_PIECES = ((0, 1, 3), (2,), (4,))
BACK_PIECES = ((4,), (0,), (1,), (2,), (3,))
STRIPES = ((0, 256), (256, 256), (512, 256), (768, 32))
SEND_DIRS = (0, 2, 5, 7, 1, 6, 3, 4)


def nn(left, right):
    return jnp.dot(left, right, preferred_element_type=F32)


def nt(left, right):
    return lax.dot_general(left, right, (((1,), (1,)), ((), ())), preferred_element_type=F32)


def parts(value, count):
    pieces = []
    for _ in range(count - 1):
        piece = value.astype(BF16)
        pieces.append(piece)
        value = value - piece.astype(F32)
    pieces.append(value.astype(BF16))
    return pieces


def iota(shape, dim):
    return lax.broadcasted_iota(jnp.int32, shape, dim)


def ones_where(mask):
    return jnp.where(mask, 1.0, 0.0).astype(F32)


def identity(size):
    return ones_where(iota((size, size), 0) == iota((size, size), 1)).astype(BF16)


def kernel(
    count_x,
    count_y,
    feat_hbm,
    cot_hbm,
    w0_hbm,
    w1_hbm,
    w2_hbm,
    w3_hbm,
    w4_hbm,
    tg_hbm,
    fg_hbm,
    harm_hbm,
    source_hbm,
    target_hbm,
    list_hbm,
    layer_ref,
    grad_ref,
    feat,
    cot,
    w0,
    w1,
    w2,
    w3,
    w4,
    tg,
    fg,
    harm,
    source_ref,
    target_ref,
    list_ref,
    feat32,
    cot32,
    outs,
    ins,
    backs,
    homes,
    mix1,
    mix2,
    mix3,
    mix4,
    harm_t,
    pick_list,
    pick_source,
    pick_source_t,
    pick_target,
    pick_target_t,
    kron_a,
    kron_at,
    kron_b,
    kron_bt,
    grid_feat,
    d_product,
    grid_agg,
    joint,
    agg,
    d_agg,
    own_t,
    local_sem,
    feat_sem,
    out_sem,
    in_sem,
    back_sem,
    home_sem,
):
    mixes = (w0, mix1, mix2, mix3, mix4)

    at_x = lax.axis_index("gx")
    at_y = lax.axis_index("gy")

    def cell(index, sign):
        step_x, step_y = DIRECTIONS[index]
        return (
            lax.rem(at_x + (sign * step_x + count_x), count_x),
            lax.rem(at_y + (sign * step_y + count_y), count_y),
        )

    def stage(buffer, order, value):
        begin, _ = PLACES[order]
        rows = SPANS[order][1]
        value = value.reshape(8, GHOST, rows)
        for at in range(0, rows - ATOMS + 1, ATOMS):
            buffer[:, begin : begin + GHOST, :] = value[:, :, at : at + ATOMS].astype(BF16)
            begin += GHOST
        if rows % ATOMS:
            left = value[:, :, rows - CH :]
            half = GHOST // 2
            buffer[:, begin : begin + half, :] = jnp.concatenate(
                [left[:, 0:half], left[:, half:]], axis=2
            ).astype(BF16)

    def staged(buffer, order):
        begin, _ = PLACES[order]
        rows = SPANS[order][1]
        tiles = []
        for _ in range(rows // ATOMS):
            tiles.append(buffer[:, begin : begin + GHOST, :].reshape(GHOSTS, ATOMS))
            begin += GHOST
        if rows % ATOMS:
            packed = buffer[:, begin : begin + GHOST // 2, :].astype(F32)
            left = jnp.concatenate([packed[:, :, 0:CH], packed[:, :, CH:]], axis=1)
            tiles.append(left.reshape(GHOSTS, CH).astype(BF16))
        return jnp.concatenate(tiles, axis=1) if len(tiles) > 1 else tiles[0]

    def exchange(piece, number, source, target, send_sem, recv_sem, sign):
        begin = PLACES[piece[0]][0]
        end = sum(PLACES[piece[-1]])
        copies = [
            pltpu.make_async_remote_copy(
                src_ref=source.at[index, begin:end],
                dst_ref=target.at[index, begin:end],
                send_sem=send_sem.at[number, index],
                recv_sem=recv_sem.at[number, index],
                device_id=cell(index, sign),
                device_id_type=MESH,
            )
            for index in SEND_DIRS
        ]
        for copy in copies:
            copy.start()
        return copies

    feat_loads = {
        order: pltpu.make_async_copy(
            feat_hbm.at[SPANS[order][0] : SPANS[order][0] + SPANS[order][1]],
            feat.at[SPANS[order][0] : SPANS[order][0] + SPANS[order][1]],
            feat_sem.at[order],
        )
        for order in range(5)
    }
    loads = [
        pltpu.make_async_copy(source, target, local_sem.at[number])
        for number, (source, target) in enumerate(
            (
                (list_hbm, list_ref),
                (source_hbm, source_ref),
                (target_hbm, target_ref),
                (harm_hbm.at[:, 0], harm),
                (tg_hbm, tg),
                (fg_hbm, fg),
                (cot_hbm, cot),
                (w0_hbm, w0),
                (w1_hbm, w1),
                (w2_hbm, w2),
                (w3_hbm, w3),
                (w4_hbm, w4),
            )
        )
    ]
    for load in (loads[0], *feat_loads.values(), *loads[1:]):
        load.start()

    barrier = pltpu.get_barrier_semaphore()
    for index in range(8):
        pl.semaphore_signal(barrier, inc=1, device_id=cell(index, 1), device_id_type=MESH)

    eye = identity(256)
    slots = ones_where(iota((GHOST, GHOSTS), 0) == (iota((GHOST, GHOSTS), 1) & 31)).astype(BF16)
    slot_rows = iota((8, GHOSTS), 0) == (iota((8, GHOSTS), 1) >> 5)
    loads[0].wait()
    list_row = nn(list_ref[...].astype(F32).astype(BF16), slots)
    list_row = jnp.sum(jnp.where(slot_rows, list_row, 0.0), axis=0, keepdims=True)
    pick_list[...] = ones_where(iota((ATOMS, GHOSTS), 0).astype(F32) == list_row).astype(BF16)
    pick_list_t = nt(eye, pick_list[...]).astype(BF16)

    lending = []
    for number, piece in enumerate(LEND_PIECES):
        for order in piece:
            first, rows = SPANS[order]
            feat_loads[order].wait()
            stage(outs, order, nt(pick_list_t, feat[first : first + rows, :]))
        if number == 0:
            pl.semaphore_wait(barrier, 8)
        lending.append(exchange(piece, number, outs, ins, out_sem, in_sem, -1))

    loads[1].wait()
    loads[2].wait()
    pick_source[...] = ones_where(
        iota((ATOMS + GHOSTS, EDGES), 0) == source_ref[...]
    ).astype(BF16)
    pick_target[...] = ones_where(iota((ATOMS, EDGES), 0) == target_ref[...]).astype(BF16)
    pick_source_t[...] = nt(eye, pick_source[...]).astype(BF16)
    pick_target_t[...] = nt(eye, pick_target[...]).astype(BF16)

    loads[3].wait()
    harm_parts = [nt(eye, piece).astype(BF16) for piece in parts(harm[...], 3)]
    for order in range(5):
        first, rows = SPANS[order]
        spread = ones_where(
            ((iota((COEFS, rows), 1) + first) >> 6) == iota((COEFS, rows), 0)
        ).astype(BF16)
        wide = nn(harm_parts[0], spread) + nn(harm_parts[1], spread) + nn(harm_parts[2], spread)
        harm_t[:, first : first + rows] = wide

    loads[4].wait()
    loads[5].wait()
    grid_rows = ones_where((iota((GRID * 8, GRID), 0) >> 3) == iota((GRID * 8, GRID), 1)).astype(BF16)
    grid_cols = ones_where((iota((GRID, GRID * 8), 1) >> 3) == iota((GRID, GRID * 8), 0)).astype(BF16)
    coef_rows = ones_where((iota((COEFS * 8, COEFS), 0) >> 3) == iota((COEFS * 8, COEFS), 1)).astype(BF16)
    coef_cols = ones_where((iota((COEFS, COEFS * 8), 1) >> 3) == iota((COEFS, COEFS * 8), 0)).astype(BF16)
    tall = (iota((GRID * 8, COEFS * 8), 0) & 7) == (iota((GRID * 8, COEFS * 8), 1) & 7)
    flat = (iota((COEFS * 8, GRID * 8), 0) & 7) == (iota((COEFS * 8, GRID * 8), 1) & 7)
    for number, (to_part, from_part) in enumerate(zip(parts(tg[...], 2), parts(fg[...], 2))):
        kron_a[number] = jnp.where(
            tall, nn(nt(grid_rows, to_part).astype(BF16), coef_cols), 0.0
        ).astype(BF16)
        kron_at[number] = jnp.where(
            flat, nn(nn(coef_rows, to_part).astype(BF16), grid_cols), 0.0
        ).astype(BF16)
        kron_b[number] = jnp.where(
            flat, nn(nn(coef_rows, from_part).astype(BF16), grid_cols), 0.0
        ).astype(BF16)
        kron_bt[number] = jnp.where(
            tall, nn(nt(grid_rows, from_part).astype(BF16), coef_cols), 0.0
        ).astype(BF16)

    feat32[...] = feat[...].astype(F32).reshape(COEFS, 8, 8, ATOMS)
    loads[6].wait()
    cot32[...] = cot[...].astype(F32).reshape(COEFS, 8, 8, ATOMS)

    def pair(ref, at):
        return jnp.concatenate(
            [ref[:, 2 * at + side].reshape(COEFS * 8, ATOMS) for side in range(2)], axis=1
        )

    def unpair(ref, at, value):
        for side in range(2):
            ref[:, 2 * at + side] = value[:, side * ATOMS : (side + 1) * ATOMS].reshape(
                COEFS, 8, ATOMS
            )

    def times(kron, value, stripe):
        high, low = parts(value, 2)
        return (
            nn(kron[0, :, stripe], high) + nn(kron[1, :, stripe], high) + nn(kron[0, :, stripe], low)
        )

    @pl.loop(0, 4)
    def _(at):
        feat_pair = pair(feat32, at).astype(BF16)
        grid_feat[at] = nn(kron_a[0], feat_pair) + nn(kron_a[1], feat_pair)
        cot_pair = pair(cot32, at).astype(BF16)
        d_product[at] = nn(kron_bt[0], cot_pair) + nn(kron_bt[1], cot_pair)
        joint[at] = (0.5 * EDGE_NORM) * grid_feat[at] * d_product[at]

    for number in range(7, 12):
        loads[number].wait()
    for weight, mix in ((w1, mix1), (w2, mix2), (w3, mix3), (w4, mix4)):
        size = weight.shape[1]
        left = ones_where(iota((size, 2 * size), 0) == iota((size, 2 * size), 1)).astype(BF16)
        right = ones_where(iota((size, 2 * size), 0) + size == iota((size, 2 * size), 1)).astype(BF16)
        mix[0:size, :] = (nn(weight[0], left) - nn(weight[1], right)).astype(BF16)
        mix[size : 2 * size, :] = (nn(weight[1], left) + nn(weight[0], right)).astype(BF16)

    for piece, copies in zip(LEND_PIECES, lending):
        ready = False
        for order in piece:
            first, rows = SPANS[order]
            columns = nt(pick_source_t[:, 0:ATOMS], feat[first : first + rows, :])
            if not ready:
                for copy in copies:
                    copy.wait_recv()
                ready = True
            columns = columns + nn(pick_source_t[:, ATOMS:], staged(ins, order))
            filtered = (columns * harm_t[:, first : first + rows]).astype(BF16)
            message = nt(mixes[order][...], filtered)
            high, low = parts(message, 2)
            total = nt(high, pick_target[...]) + nt(low, pick_target[...])
            agg[first // CH : (first + rows) // CH] = (total * (0.5 * EDGE_NORM)).reshape(
                rows // CH, 8, 8, ATOMS
            )

    ahead = [(at, begin, size) for at in range(4) for begin, size in STRIPES]

    def first_product(at, begin, size):
        return nn(kron_a[0, begin : begin + size, :], pair(agg, at).astype(BF16))

    rough_next = first_product(*ahead[0])
    for step, (at, begin, size) in enumerate(ahead):
        rough = rough_next
        if step + 1 < len(ahead):
            rough_next = first_product(*ahead[step + 1])
        stripe = slice(begin, begin + size)
        grid_agg[at, stripe, :] = rough
        turn = jnp.tanh(rough)
        slope = (1.0 + turn) * (1.0 + rough * (1.0 - turn))
        term = nn(kron_at[0, :, stripe], (joint[at, stripe, :] * slope).astype(BF16))
        total = term if begin == 0 else total + term
        if step + 1 == len(ahead) or ahead[step + 1][0] != at:
            unpair(d_agg, at, total)

    returning = []
    for number, piece in enumerate(BACK_PIECES):
        order = piece[0]
        first, rows = SPANS[order]
        d_rows = d_agg[first // CH : (first + rows) // CH].reshape(rows, ATOMS).astype(BF16)
        d_message = nt(pick_target_t[...], d_rows).astype(BF16)
        d_filtered = nn(d_message, mixes[order][...])
        high, low = parts(d_filtered * harm_t[:, first : first + rows], 2)
        ghosts = nn(pick_source[ATOMS:, :], high)
        stage(backs, order, ghosts)
        returning.append(exchange(piece, number, backs, homes, back_sem, home_sem, 1))
        own_t[:, first : first + rows] = nn(pick_source[0:ATOMS, :], high) + nn(
            pick_source[0:ATOMS, :], low
        )

    @pl.loop(0, 4)
    def _(at):
        agg_high, agg_low = parts(pair(agg, at), 2)
        update = None
        for begin, size in STRIPES:
            stripe = slice(begin, begin + size)
            exact = (
                grid_agg[at, stripe, :]
                + nn(kron_a[1, stripe, :], agg_high)
                + nn(kron_a[0, stripe, :], agg_low)
            )
            exact = exact + exact
            active = exact * jax.nn.sigmoid(exact)
            made = times(kron_b, active * grid_feat[at, stripe, :], stripe)
            back = times(kron_at, active * d_product[at, stripe, :], stripe)
            update = made if update is None else update + made
            d_node = back if begin == 0 else d_node + back
        unpair(feat32, at, pair(feat32, at) + update)
        unpair(cot32, at, pair(cot32, at) + d_node)

    layer_ref[...] = feat32[...].reshape(ROWS, ATOMS).astype(BF16)

    for (order,), copies in zip(BACK_PIECES, returning):
        first, rows = SPANS[order]
        for copy in copies:
            copy.wait_recv()
        arrived = staged(homes, order)
        total = own_t[:, first : first + rows] + nn(pick_list[...], arrived)
        node = cot32[first // CH : (first + rows) // CH].reshape(rows, ATOMS)
        grad_ref[first : first + rows, :] = node + jnp.transpose(total)

    for copies in (*lending, *returning):
        for copy in copies:
            copy.wait_send()


def store_kernel(layer_ref, grad_ref, layer_hbm, grad_hbm, sem):
    copies = [
        pltpu.make_async_copy(layer_ref, layer_hbm, sem.at[0]),
        pltpu.make_async_copy(grad_ref, grad_hbm, sem.at[1]),
    ]
    for copy in copies:
        copy.start()
    for copy in copies:
        copy.wait()


def per_device(
    features,
    cotangent,
    w_order0,
    w_order1,
    w_order2,
    w_order3,
    w_order4,
    to_grid,
    from_grid,
    edge_harmonics,
    edge_source,
    edge_target,
    send_list,
):
    count_x = lax.axis_size("gx")
    count_y = lax.axis_size("gy")
    in_hbm = pl.BlockSpec(memory_space=pltpu.HBM)
    vmem = pl.BlockSpec(memory_space=pltpu.VMEM)
    grids = pltpu.VMEM((4, GRID * 8, 2 * ATOMS), F32)
    tiles = pltpu.VMEM((COEFS, 8, 8, ATOMS), F32)
    tall = pltpu.VMEM((2, GRID * 8, COEFS * 8), BF16)
    flat = pltpu.VMEM((2, COEFS * 8, GRID * 8), BF16)
    blocks = pltpu.VMEM((8, WIRE, ATOMS), BF16)
    lend_sems = pltpu.SemaphoreType.DMA((len(LEND_PIECES), 8))
    back_sems = pltpu.SemaphoreType.DMA((len(BACK_PIECES), 8))
    layer, grad = pl.pallas_call(
        functools.partial(kernel, count_x, count_y),
        out_shape=(
            jax.ShapeDtypeStruct((ROWS, ATOMS), BF16),
            jax.ShapeDtypeStruct((ROWS, ATOMS), F32),
        ),
        in_specs=[in_hbm] * 13,
        out_specs=(vmem, vmem),
        scratch_shapes=[
            pltpu.VMEM((ROWS, ATOMS), BF16),
            pltpu.VMEM((ROWS, ATOMS), BF16),
            pltpu.VMEM(w_order0.shape, BF16),
            pltpu.VMEM(w_order1.shape, BF16),
            pltpu.VMEM(w_order2.shape, BF16),
            pltpu.VMEM(w_order3.shape, BF16),
            pltpu.VMEM(w_order4.shape, BF16),
            pltpu.VMEM((COEFS, GRID), F32),
            pltpu.VMEM((COEFS, GRID), F32),
            pltpu.VMEM((COEFS, EDGES), F32),
            pltpu.VMEM((1, EDGES), jnp.int32),
            pltpu.VMEM((1, EDGES), jnp.int32),
            pltpu.VMEM((8, GHOST), jnp.int32),
            tiles,
            tiles,
            blocks,
            blocks,
            blocks,
            blocks,
            *[pltpu.VMEM((rows, rows), BF16) for _, rows in SPANS[1:]],
            pltpu.VMEM((EDGES, ROWS), F32),
            pltpu.VMEM((ATOMS, GHOSTS), BF16),
            pltpu.VMEM((ATOMS + GHOSTS, EDGES), BF16),
            pltpu.VMEM((EDGES, ATOMS + GHOSTS), BF16),
            pltpu.VMEM((ATOMS, EDGES), BF16),
            pltpu.VMEM((EDGES, ATOMS), BF16),
            tall,
            flat,
            flat,
            tall,
            grids,
            grids,
            grids,
            grids,
            tiles,
            tiles,
            pltpu.VMEM((ATOMS, ROWS), F32),
            pltpu.SemaphoreType.DMA((12,)),
            pltpu.SemaphoreType.DMA((5,)),
            lend_sems,
            lend_sems,
            back_sems,
            back_sems,
        ],
        compiler_params=pltpu.CompilerParams(
            collective_id=0, has_side_effects=True, vmem_limit_bytes=40 * 1024 * 1024
        ),
        name="layer",
    )(
        *[
            pltpu.with_memory_space_constraint(value, pltpu.HBM)
            for value in (
                features[0, 0],
                cotangent[0, 0],
                w_order0,
                w_order1,
                w_order2,
                w_order3,
                w_order4,
                to_grid.T,
                from_grid,
                edge_harmonics[0, 0].reshape(COEFS, 1, EDGES),
                edge_source[0],
                edge_target[0],
                send_list[0, 0],
            )
        ],
    )
    layer, grad = pl.pallas_call(
        store_kernel,
        out_shape=(
            jax.ShapeDtypeStruct((ROWS, ATOMS), BF16),
            jax.ShapeDtypeStruct((ROWS, ATOMS), F32),
        ),
        in_specs=[vmem, vmem],
        out_specs=(in_hbm, in_hbm),
        scratch_shapes=[pltpu.SemaphoreType.DMA((2,))],
        compiler_params=pltpu.CompilerParams(vmem_limit_bytes=4 * 1024 * 1024),
        name="store",
    )(layer, grad)
    return layer[None, None], grad[None, None]


def solution(mesh):
    cells = P("gx", "gy", None, None)
    placed = (cells, cells, P(), P(), P(), P(), P(), P(), P(), cells, P("gx", "gy", None), P("gx", "gy", None), cells)
    return jax.shard_map(
        per_device,
        mesh=mesh,
        in_specs=placed,
        out_specs=(cells, cells),
        check_vma=False,
    )
```

```python
import functools

import jax
import jax.numpy as jnp
from jax import lax
from jax.experimental import pallas as pl
from jax.experimental.pallas import tpu as pltpu
from jax.sharding import PartitionSpec as P

DIRECTIONS = ((-1, -1), (-1, 0), (-1, 1), (0, -1), (0, 1), (1, -1), (1, 0), (1, 1))
EDGE_NORM = 0.35
MESH = pl.DeviceIdType.MESH
F32 = jnp.float32
BF16 = jnp.bfloat16

COEFS = 25
CH = 64
GRID = 100
ATOMS = 128
EDGES = 256
GHOST = 32
ROWS = COEFS * CH
GHOSTS = 8 * GHOST
SPANS = ((0, 320), (320, 512), (832, 384), (1216, 256), (1472, 128))
PLACES = ((0, 80), (80, 128), (272, 96), (208, 64), (368, 32))
WIRE = 400
LEND_PIECES = ((0, 1, 3), (2,), (4,))
BACK_PIECES = ((4,), (0,), (1,), (2,), (3,))
STRIPES = ((0, 256), (256, 256), (512, 256), (768, 32))
SEND_DIRS = (0, 2, 5, 7, 1, 6, 3, 4)


def nn(left, right):
    return jnp.dot(left, right, preferred_element_type=F32)


def nt(left, right):
    return lax.dot_general(left, right, (((1,), (1,)), ((), ())), preferred_element_type=F32)


def parts(value, count):
    pieces = []
    for _ in range(count - 1):
        piece = value.astype(BF16)
        pieces.append(piece)
        value = value - piece.astype(F32)
    pieces.append(value.astype(BF16))
    return pieces


def iota(shape, dim):
    return lax.broadcasted_iota(jnp.int32, shape, dim)


def ones_where(mask):
    return jnp.where(mask, 1.0, 0.0).astype(F32)


def identity(size):
    return ones_where(iota((size, size), 0) == iota((size, size), 1)).astype(BF16)


def kernel(
    count_x,
    count_y,
    feat_hbm,
    cot_hbm,
    w0_hbm,
    w1_hbm,
    w2_hbm,
    w3_hbm,
    w4_hbm,
    tg_hbm,
    fg_hbm,
    harm_hbm,
    source_hbm,
    target_hbm,
    list_hbm,
    layer_ref,
    grad_ref,
    feat,
    cot,
    w0,
    w1,
    w2,
    w3,
    w4,
    tg,
    fg,
    harm,
    source_ref,
    target_ref,
    list_ref,
    feat32,
    cot32,
    outs,
    ins,
    backs,
    homes,
    mix1,
    mix2,
    mix3,
    mix4,
    harm_t,
    pick_list,
    pick_source,
    pick_source_t,
    pick_target,
    pick_target_t,
    kron_a,
    kron_at,
    kron_b,
    kron_bt,
    grid_feat,
    d_product,
    grid_agg,
    joint,
    agg,
    d_agg,
    own_t,
    local_sem,
    feat_sem,
    out_sem,
    in_sem,
    back_sem,
    home_sem,
):
    mixes = (w0, mix1, mix2, mix3, mix4)

    at_x = lax.axis_index("gx")
    at_y = lax.axis_index("gy")

    def cell(index, sign):
        step_x, step_y = DIRECTIONS[index]
        return (
            lax.rem(at_x + (sign * step_x + count_x), count_x),
            lax.rem(at_y + (sign * step_y + count_y), count_y),
        )

    def stage(buffer, order, value):
        begin, _ = PLACES[order]
        rows = SPANS[order][1]
        value = value.reshape(8, GHOST, rows)
        for at in range(0, rows - ATOMS + 1, ATOMS):
            buffer[:, begin : begin + GHOST, :] = value[:, :, at : at + ATOMS].astype(BF16)
            begin += GHOST
        if rows % ATOMS:
            left = value[:, :, rows - CH :]
            half = GHOST // 2
            buffer[:, begin : begin + half, :] = jnp.concatenate(
                [left[:, 0:half], left[:, half:]], axis=2
            ).astype(BF16)

    def staged(buffer, order):
        begin, _ = PLACES[order]
        rows = SPANS[order][1]
        tiles = []
        for _ in range(rows // ATOMS):
            tiles.append(buffer[:, begin : begin + GHOST, :].reshape(GHOSTS, ATOMS))
            begin += GHOST
        if rows % ATOMS:
            packed = buffer[:, begin : begin + GHOST // 2, :].astype(F32)
            left = jnp.concatenate([packed[:, :, 0:CH], packed[:, :, CH:]], axis=1)
            tiles.append(left.reshape(GHOSTS, CH).astype(BF16))
        return jnp.concatenate(tiles, axis=1) if len(tiles) > 1 else tiles[0]

    def exchange(piece, number, source, target, send_sem, recv_sem, sign):
        begin = PLACES[piece[0]][0]
        end = sum(PLACES[piece[-1]])
        copies = [
            pltpu.make_async_remote_copy(
                src_ref=source.at[index, begin:end],
                dst_ref=target.at[index, begin:end],
                send_sem=send_sem.at[number, index],
                recv_sem=recv_sem.at[number, index],
                device_id=cell(index, sign),
                device_id_type=MESH,
            )
            for index in SEND_DIRS
        ]
        for copy in copies:
            copy.start()
        return copies

    feat_loads = {
        order: pltpu.make_async_copy(
            feat_hbm.at[SPANS[order][0] : SPANS[order][0] + SPANS[order][1]],
            feat.at[SPANS[order][0] : SPANS[order][0] + SPANS[order][1]],
            feat_sem.at[order],
        )
        for order in range(5)
    }
    loads = [
        pltpu.make_async_copy(source, target, local_sem.at[number])
        for number, (source, target) in enumerate(
            (
                (list_hbm, list_ref),
                (source_hbm, source_ref),
                (target_hbm, target_ref),
                (harm_hbm.at[:, 0], harm),
                (tg_hbm, tg),
                (fg_hbm, fg),
                (cot_hbm, cot),
                (w0_hbm, w0),
                (w1_hbm, w1),
                (w2_hbm, w2),
                (w3_hbm, w3),
                (w4_hbm, w4),
            )
        )
    ]
    for load in (loads[0], *feat_loads.values(), *loads[1:]):
        load.start()

    barrier = pltpu.get_barrier_semaphore()
    for index in range(8):
        pl.semaphore_signal(barrier, inc=1, device_id=cell(index, 1), device_id_type=MESH)

    eye = identity(256)
    slots = ones_where(iota((GHOST, GHOSTS), 0) == (iota((GHOST, GHOSTS), 1) & 31)).astype(BF16)
    slot_rows = iota((8, GHOSTS), 0) == (iota((8, GHOSTS), 1) >> 5)
    loads[0].wait()
    list_row = nn(list_ref[...].astype(F32).astype(BF16), slots)
    list_row = jnp.sum(jnp.where(slot_rows, list_row, 0.0), axis=0, keepdims=True)
    pick_list[...] = ones_where(iota((ATOMS, GHOSTS), 0).astype(F32) == list_row).astype(BF16)
    pick_list_t = nt(eye, pick_list[...]).astype(BF16)

    lending = []
    for number, piece in enumerate(LEND_PIECES):
        for order in piece:
            first, rows = SPANS[order]
            feat_loads[order].wait()
            stage(outs, order, nt(pick_list_t, feat[first : first + rows, :]))
        if number == 0:
            pl.semaphore_wait(barrier, 8)
        lending.append(exchange(piece, number, outs, ins, out_sem, in_sem, -1))

    loads[1].wait()
    loads[2].wait()
    pick_source[...] = ones_where(
        iota((ATOMS + GHOSTS, EDGES), 0) == source_ref[...]
    ).astype(BF16)
    pick_target[...] = ones_where(iota((ATOMS, EDGES), 0) == target_ref[...]).astype(BF16)
    pick_source_t[...] = nt(eye, pick_source[...]).astype(BF16)
    pick_target_t[...] = nt(eye, pick_target[...]).astype(BF16)

    loads[3].wait()
    harm_parts = [nt(eye, piece).astype(BF16) for piece in parts(harm[...], 3)]
    for order in range(5):
        first, rows = SPANS[order]
        spread = ones_where(
            ((iota((COEFS, rows), 1) + first) >> 6) == iota((COEFS, rows), 0)
        ).astype(BF16)
        wide = nn(harm_parts[0], spread) + nn(harm_parts[1], spread) + nn(harm_parts[2], spread)
        harm_t[:, first : first + rows] = wide

    loads[4].wait()
    loads[5].wait()
    grid_rows = ones_where((iota((GRID * 8, GRID), 0) >> 3) == iota((GRID * 8, GRID), 1)).astype(BF16)
    grid_cols = ones_where((iota((GRID, GRID * 8), 1) >> 3) == iota((GRID, GRID * 8), 0)).astype(BF16)
    coef_rows = ones_where((iota((COEFS * 8, COEFS), 0) >> 3) == iota((COEFS * 8, COEFS), 1)).astype(BF16)
    coef_cols = ones_where((iota((COEFS, COEFS * 8), 1) >> 3) == iota((COEFS, COEFS * 8), 0)).astype(BF16)
    tall = (iota((GRID * 8, COEFS * 8), 0) & 7) == (iota((GRID * 8, COEFS * 8), 1) & 7)
    flat = (iota((COEFS * 8, GRID * 8), 0) & 7) == (iota((COEFS * 8, GRID * 8), 1) & 7)
    for number, (to_part, from_part) in enumerate(zip(parts(tg[...], 2), parts(fg[...], 2))):
        kron_a[number] = jnp.where(
            tall, nn(nt(grid_rows, to_part).astype(BF16), coef_cols), 0.0
        ).astype(BF16)
        kron_at[number] = jnp.where(
            flat, nn(nn(coef_rows, to_part).astype(BF16), grid_cols), 0.0
        ).astype(BF16)
        kron_b[number] = jnp.where(
            flat, nn(nn(coef_rows, from_part).astype(BF16), grid_cols), 0.0
        ).astype(BF16)
        kron_bt[number] = jnp.where(
            tall, nn(nt(grid_rows, from_part).astype(BF16), coef_cols), 0.0
        ).astype(BF16)

    feat32[...] = feat[...].astype(F32).reshape(COEFS, 8, 8, ATOMS)
    loads[6].wait()
    cot32[...] = cot[...].astype(F32).reshape(COEFS, 8, 8, ATOMS)

    def pair(ref, at):
        return jnp.concatenate(
            [ref[:, 2 * at + side].reshape(COEFS * 8, ATOMS) for side in range(2)], axis=1
        )

    def unpair(ref, at, value):
        for side in range(2):
            ref[:, 2 * at + side] = value[:, side * ATOMS : (side + 1) * ATOMS].reshape(
                COEFS, 8, ATOMS
            )

    def times(kron, value, stripe):
        high, low = parts(value, 2)
        return (
            nn(kron[0, :, stripe], high) + nn(kron[1, :, stripe], high) + nn(kron[0, :, stripe], low)
        )

    for at in range(4):
        feat_pair = pair(feat32, at).astype(BF16)
        grid_feat[at] = nn(kron_a[0], feat_pair) + nn(kron_a[1], feat_pair)
        cot_pair = pair(cot32, at).astype(BF16)
        d_product[at] = nn(kron_bt[0], cot_pair) + nn(kron_bt[1], cot_pair)
        joint[at] = (0.5 * EDGE_NORM) * grid_feat[at] * d_product[at]

    for number in range(7, 12):
        loads[number].wait()
    for weight, mix in ((w1, mix1), (w2, mix2), (w3, mix3), (w4, mix4)):
        size = weight.shape[1]
        left = ones_where(iota((size, 2 * size), 0) == iota((size, 2 * size), 1)).astype(BF16)
        right = ones_where(iota((size, 2 * size), 0) + size == iota((size, 2 * size), 1)).astype(BF16)
        mix[0:size, :] = (nn(weight[0], left) - nn(weight[1], right)).astype(BF16)
        mix[size : 2 * size, :] = (nn(weight[1], left) + nn(weight[0], right)).astype(BF16)

    for piece, copies in zip(LEND_PIECES, lending):
        ready = False
        for order in piece:
            first, rows = SPANS[order]
            columns = nt(pick_source_t[:, 0:ATOMS], feat[first : first + rows, :])
            if not ready:
                for copy in copies:
                    copy.wait_recv()
                ready = True
            columns = columns + nn(pick_source_t[:, ATOMS:], staged(ins, order))
            filtered = (columns * harm_t[:, first : first + rows]).astype(BF16)
            message = nt(mixes[order][...], filtered)
            high, low = parts(message, 2)
            total = nt(high, pick_target[...]) + nt(low, pick_target[...])
            agg[first // CH : (first + rows) // CH] = (total * (0.5 * EDGE_NORM)).reshape(
                rows // CH, 8, 8, ATOMS
            )

    ahead = [(at, begin, size) for at in range(4) for begin, size in STRIPES]

    def first_product(at, begin, size):
        return nn(kron_a[0, begin : begin + size, :], pair(agg, at).astype(BF16))

    rough_next = first_product(*ahead[0])
    for step, (at, begin, size) in enumerate(ahead):
        rough = rough_next
        if step + 1 < len(ahead):
            rough_next = first_product(*ahead[step + 1])
        stripe = slice(begin, begin + size)
        grid_agg[at, stripe, :] = rough
        turn = jnp.tanh(rough)
        slope = (1.0 + turn) * (1.0 + rough * (1.0 - turn))
        term = nn(kron_at[0, :, stripe], (joint[at, stripe, :] * slope).astype(BF16))
        total = term if begin == 0 else total + term
        if step + 1 == len(ahead) or ahead[step + 1][0] != at:
            unpair(d_agg, at, total)

    returning = []
    for number, piece in enumerate(BACK_PIECES):
        order = piece[0]
        first, rows = SPANS[order]
        d_rows = d_agg[first // CH : (first + rows) // CH].reshape(rows, ATOMS).astype(BF16)
        d_message = nt(pick_target_t[...], d_rows).astype(BF16)
        d_filtered = nn(d_message, mixes[order][...])
        high, low = parts(d_filtered * harm_t[:, first : first + rows], 2)
        ghosts = nn(pick_source[ATOMS:, :], high)
        stage(backs, order, ghosts)
        returning.append(exchange(piece, number, backs, homes, back_sem, home_sem, 1))
        own_t[:, first : first + rows] = nn(pick_source[0:ATOMS, :], high) + nn(
            pick_source[0:ATOMS, :], low
        )

    @pl.loop(0, 4)
    def _(at):
        agg_high, agg_low = parts(pair(agg, at), 2)
        update = None
        for begin, size in STRIPES:
            stripe = slice(begin, begin + size)
            exact = (
                grid_agg[at, stripe, :]
                + nn(kron_a[1, stripe, :], agg_high)
                + nn(kron_a[0, stripe, :], agg_low)
            )
            exact = exact + exact
            active = exact * jax.nn.sigmoid(exact)
            made = times(kron_b, active * grid_feat[at, stripe, :], stripe)
            back = times(kron_at, active * d_product[at, stripe, :], stripe)
            update = made if update is None else update + made
            d_node = back if begin == 0 else d_node + back
        unpair(feat32, at, pair(feat32, at) + update)
        unpair(cot32, at, pair(cot32, at) + d_node)

    layer_ref[...] = feat32[...].reshape(ROWS, ATOMS).astype(BF16)

    for (order,), copies in zip(BACK_PIECES, returning):
        first, rows = SPANS[order]
        for copy in copies:
            copy.wait_recv()
        arrived = staged(homes, order)
        total = own_t[:, first : first + rows] + nn(pick_list[...], arrived)
        node = cot32[first // CH : (first + rows) // CH].reshape(rows, ATOMS)
        grad_ref[first : first + rows, :] = node + jnp.transpose(total)

    for copies in (*lending, *returning):
        for copy in copies:
            copy.wait_send()


def store_kernel(layer_ref, grad_ref, layer_hbm, grad_hbm, sem):
    copies = [
        pltpu.make_async_copy(layer_ref, layer_hbm, sem.at[0]),
        pltpu.make_async_copy(grad_ref, grad_hbm, sem.at[1]),
    ]
    for copy in copies:
        copy.start()
    for copy in copies:
        copy.wait()


def per_device(
    features,
    cotangent,
    w_order0,
    w_order1,
    w_order2,
    w_order3,
    w_order4,
    to_grid,
    from_grid,
    edge_harmonics,
    edge_source,
    edge_target,
    send_list,
):
    count_x = lax.axis_size("gx")
    count_y = lax.axis_size("gy")
    in_hbm = pl.BlockSpec(memory_space=pltpu.HBM)
    vmem = pl.BlockSpec(memory_space=pltpu.VMEM)
    grids = pltpu.VMEM((4, GRID * 8, 2 * ATOMS), F32)
    tiles = pltpu.VMEM((COEFS, 8, 8, ATOMS), F32)
    tall = pltpu.VMEM((2, GRID * 8, COEFS * 8), BF16)
    flat = pltpu.VMEM((2, COEFS * 8, GRID * 8), BF16)
    blocks = pltpu.VMEM((8, WIRE, ATOMS), BF16)
    lend_sems = pltpu.SemaphoreType.DMA((len(LEND_PIECES), 8))
    back_sems = pltpu.SemaphoreType.DMA((len(BACK_PIECES), 8))
    layer, grad = pl.pallas_call(
        functools.partial(kernel, count_x, count_y),
        out_shape=(
            jax.ShapeDtypeStruct((ROWS, ATOMS), BF16),
            jax.ShapeDtypeStruct((ROWS, ATOMS), F32),
        ),
        in_specs=[in_hbm] * 13,
        out_specs=(vmem, vmem),
        scratch_shapes=[
            pltpu.VMEM((ROWS, ATOMS), BF16),
            pltpu.VMEM((ROWS, ATOMS), BF16),
            pltpu.VMEM(w_order0.shape, BF16),
            pltpu.VMEM(w_order1.shape, BF16),
            pltpu.VMEM(w_order2.shape, BF16),
            pltpu.VMEM(w_order3.shape, BF16),
            pltpu.VMEM(w_order4.shape, BF16),
            pltpu.VMEM((COEFS, GRID), F32),
            pltpu.VMEM((COEFS, GRID), F32),
            pltpu.VMEM((COEFS, EDGES), F32),
            pltpu.VMEM((1, EDGES), jnp.int32),
            pltpu.VMEM((1, EDGES), jnp.int32),
            pltpu.VMEM((8, GHOST), jnp.int32),
            tiles,
            tiles,
            blocks,
            blocks,
            blocks,
            blocks,
            *[pltpu.VMEM((rows, rows), BF16) for _, rows in SPANS[1:]],
            pltpu.VMEM((EDGES, ROWS), F32),
            pltpu.VMEM((ATOMS, GHOSTS), BF16),
            pltpu.VMEM((ATOMS + GHOSTS, EDGES), BF16),
            pltpu.VMEM((EDGES, ATOMS + GHOSTS), BF16),
            pltpu.VMEM((ATOMS, EDGES), BF16),
            pltpu.VMEM((EDGES, ATOMS), BF16),
            tall,
            flat,
            flat,
            tall,
            grids,
            grids,
            grids,
            grids,
            tiles,
            tiles,
            pltpu.VMEM((ATOMS, ROWS), F32),
            pltpu.SemaphoreType.DMA((12,)),
            pltpu.SemaphoreType.DMA((5,)),
            lend_sems,
            lend_sems,
            back_sems,
            back_sems,
        ],
        compiler_params=pltpu.CompilerParams(
            collective_id=0, has_side_effects=True, vmem_limit_bytes=40 * 1024 * 1024
        ),
        name="layer",
    )(
        *[
            pltpu.with_memory_space_constraint(value, pltpu.HBM)
            for value in (
                features[0, 0],
                cotangent[0, 0],
                w_order0,
                w_order1,
                w_order2,
                w_order3,
                w_order4,
                to_grid.T,
                from_grid,
                edge_harmonics[0, 0].reshape(COEFS, 1, EDGES),
                edge_source[0],
                edge_target[0],
                send_list[0, 0],
            )
        ],
    )
    layer, grad = pl.pallas_call(
        store_kernel,
        out_shape=(
            jax.ShapeDtypeStruct((ROWS, ATOMS), BF16),
            jax.ShapeDtypeStruct((ROWS, ATOMS), F32),
        ),
        in_specs=[vmem, vmem],
        out_specs=(in_hbm, in_hbm),
        scratch_shapes=[pltpu.SemaphoreType.DMA((2,))],
        compiler_params=pltpu.CompilerParams(vmem_limit_bytes=4 * 1024 * 1024),
        name="store",
    )(layer, grad)
    return layer[None, None], grad[None, None]


def solution(mesh):
    cells = P("gx", "gy", None, None)
    placed = (cells, cells, P(), P(), P(), P(), P(), P(), P(), cells, P("gx", "gy", None), P("gx", "gy", None), cells)
    return jax.shard_map(
        per_device,
        mesh=mesh,
        in_specs=placed,
        out_specs=(cells, cells),
        check_vma=False,
    )
```
